128 devices in a mesh: elem: 128 (over x, y, z, core).
Axes of the slice: x: 4, y: 4, z: 4, core: 2. Of those that a mesh axis runs over, the one named last changes fastest.
Arguments:
- elem_mats: bfloat16 [1536, 750, 750], P('elem'), may hold values from -0.14 to 0.64
- face_blocks: bfloat16 [3456, 125, 125], P('elem'), may hold values from -0.45 to 1.25
- rhs: bfloat16 [3456, 16, 125], P('elem'), may hold values from -6 to 6
- elem_faces: int32 [1536, 6], replicated, may hold values from 0 to 3455, as said below
- orient: int32 [1536, 6], replicated, may hold values from 0 to 7
- counts: int32 [128], replicated, may hold values from 3 to 9, as said below
Outputs:
- traces: float32 [3456, 16, 125], P('elem')
The draws below stay inside these ranges and needn't reach their ends.
Inputs may be any that keep to these rules, and one draw needn't show every extreme that they name: Element slots 0 to counts[d] - 1 of device d (rows d * 12 onward) are live, the others empty; counts[2 i] + counts[2 i + 1] = 12. `elem_faces`: face f is owned by device f // 27. A live element slot of device d has all its faces owned by devices d - 2 to d + 2; device d has exactly 4 live element faces owned by each other device within that distance; a face is listed by at most two live element faces. Rows of empty slots hold arbitrary faces.
All inputs are finite; a program needn't handle non-finite values.
Results may differ from the reference program's by a relative error of at most 0.0017.
Values may be sent and summed in bfloat16 or wider, within the bound.
A program may use at most 128 MiB of HBM per device.

```python
import math
import jax
import jax.numpy as jnp
import numpy as np
from jax import lax

COMP = 5
EDGE = 5
NFUN = 16
E_CAP = 12
ITERS = 2
REACH = 2
TRACE = 125
DOF = 750
SLOT = 4
FACE_DEV = 27
NELEM = 1536
FACES = 3456
N_ELEM = 128


def build_layout(key):
    lowest = E_CAP // 4
    pair_total = N_ELEM // 2
    per_device = 6 * E_CAP
    total_slots = N_ELEM * per_device
    heavier = jax.random.randint(jax.random.fold_in(key, 101), (pair_total,), E_CAP // 2, E_CAP - lowest + 1)
    extreme = jax.random.randint(jax.random.fold_in(key, 102), (), 0, pair_total)
    heavier = jnp.where(jnp.arange(pair_total) == extreme, E_CAP - lowest, heavier)
    flipped = jax.random.randint(jax.random.fold_in(key, 103), (pair_total,), 0, 2)
    even_count = jnp.where(flipped == 0, heavier, E_CAP - heavier)
    counts = jnp.stack([even_count, E_CAP - even_count], axis=1).reshape(N_ELEM).astype(jnp.int32)
    device_of = jnp.arange(total_slots, dtype=jnp.int32) // per_device
    slot_of = jnp.arange(total_slots, dtype=jnp.int32) % per_device
    is_live = slot_of // 6 < counts[device_of]
    scores = jax.random.randint(jax.random.fold_in(key, 104), (total_slots,), 0, 1 << 20) * per_device + slot_of
    scores = jnp.where(is_live, scores, scores + (1 << 30))
    order_in = jnp.argsort(scores.reshape(N_ELEM, per_device), axis=1)
    rank_in = jnp.argsort(order_in, axis=1).reshape(total_slots).astype(jnp.int32)
    offsets = jnp.array(list(range(1, REACH + 1)) + [-step_size for step_size in range(1, REACH + 1)], jnp.int32)
    bucket = rank_in // SLOT
    offset_of = offsets[jnp.clip(bucket, 0, 2 * REACH - 1)]
    target = device_of + offset_of
    sending = is_live & (bucket < 2 * REACH) & (target >= 0) & (target < N_ELEM)
    target = jnp.where(sending, target, device_of)
    group_of = jnp.where(is_live, target, N_ELEM)
    shuffled = jax.random.permutation(jax.random.fold_in(key, 105), total_slots)
    sorted_pos = shuffled[jnp.argsort(group_of[shuffled], stable=True)]
    group_sizes = jnp.zeros((N_ELEM + 1,), jnp.int32).at[group_of].add(1)
    starts = jnp.cumsum(group_sizes) - group_sizes
    position = jnp.arange(total_slots, dtype=jnp.int32) - starts[group_of[sorted_pos]]
    place_in = jnp.zeros((total_slots,), jnp.int32).at[sorted_pos].set(position)
    face_ids = jnp.where(is_live, target * FACE_DEV + place_in // 2, device_of * FACE_DEV)
    return (counts, face_ids.reshape(N_ELEM * E_CAP, 6).astype(jnp.int32))


def draw_counts(key, part):
    return build_layout(key)[0]


def draw_elem_faces(key, part):
    return build_layout(key)[1]


def draw_elem_mats(key, part):
    shape = (N_ELEM * E_CAP, DOF, DOF)
    noise = jax.random.truncated_normal(key, -6.0, 6.0, shape, jnp.float32)
    return (0.5 * jnp.eye(DOF, dtype=jnp.float32) + 0.15 / math.sqrt(DOF) * noise).astype(jnp.bfloat16)


def draw_face_blocks(key, part):
    shape = (FACE_DEV * N_ELEM, TRACE, TRACE)
    noise = jax.random.truncated_normal(key, -6.0, 6.0, shape, jnp.float32)
    return (0.8 * jnp.eye(TRACE, dtype=jnp.float32) + 0.2 / math.sqrt(TRACE) * noise).astype(jnp.bfloat16)


def place_ends(entries, key, smallest, high):
    longest = entries.shape.index(max(entries.shape))
    spots = []
    for shift in (0, 1):
        where = [jax.random.randint(jax.random.fold_in(key, axis), (), 0, length) for axis, length in enumerate(entries.shape)]
        where[longest] = (where[longest] + shift) % entries.shape[longest]
        spots.append(tuple(where))
    return entries.at[spots[0]].set(smallest).at[spots[1]].set(high)


def block_levels(key, dims, shards, least, largest):
    level, own = 1.0, jax.random.fold_in(key, 6)
    for axis_at, parts in shards:
        draws = jnp.exp(jax.random.uniform(jax.random.fold_in(own, axis_at), (parts,), jnp.float32, least / len(shards), largest / len(shards)))
        level = level * jnp.repeat(draws, dims[axis_at] // parts).reshape([-1 if axis == axis_at else 1 for axis in range(len(dims))])
    return level


def gaussian(key, dims, spread, reach, split=(), kind=jnp.bfloat16):
    gain = block_levels(key, dims, split, -0.22, 0.18) if split else 1.0
    values = jax.random.normal(key, dims, jnp.float32) * spread * gain
    return jnp.minimum(jnp.maximum(values, -reach), reach).astype(kind)


def setup_inputs(seed: int = 0) -> dict:
    arg_keys = jax.random.split(jax.random.key(seed), 7)
    elem_mats = draw_elem_mats(jax.random.fold_in(arg_keys[6], 71), 0)
    face_blocks = draw_face_blocks(jax.random.fold_in(arg_keys[6], 71), 0)
    rhs = gaussian(arg_keys[2], (FACES, NFUN, TRACE), 1.0, 6.0, ((0, 128),))
    elem_faces = draw_elem_faces(jax.random.fold_in(arg_keys[6], 71), 0)
    orient = place_ends(jax.random.randint(arg_keys[4], (NELEM, 6), 0, 8), jax.random.fold_in(arg_keys[4], 1), 0, 7).astype(jnp.int32)
    counts = draw_counts(jax.random.fold_in(arg_keys[6], 71), 0)
    return dict(elem_mats=elem_mats, face_blocks=face_blocks, rhs=rhs, elem_faces=elem_faces, orient=orient, counts=counts)


def orient_tables(edge_nodes, components):
    node_ids = np.arange(edge_nodes * edge_nodes)
    row_pos = node_ids // edge_nodes
    col_pos = node_ids % edge_nodes
    table_rows = []
    for orient_code in range(8):
        if orient_code & 4:
            first_pos, second_pos = col_pos, row_pos
        else:
            first_pos, second_pos = row_pos, col_pos
        if orient_code & 1:
            first_pos = edge_nodes - 1 - first_pos
        if orient_code & 2:
            second_pos = edge_nodes - 1 - second_pos
        moved_node = first_pos * edge_nodes + second_pos
        table_rows.append(np.concatenate([part_index * edge_nodes * edge_nodes + moved_node for part_index in range(components)]))
    forward = np.stack(table_rows).astype(np.int32)
    backward = np.argsort(forward, axis=1).astype(np.int32)
    return forward, backward


def per_device(operands):
    traces_block, matrix_block = operands
    return jnp.einsum("akni,akilj->alnj", traces_block.astype(jnp.float32), matrix_block.astype(jnp.float32))


def reference(elem_mats, face_blocks, rhs, elem_faces, orient, counts):
    forward, backward = orient_tables(EDGE, COMP)
    to_element = jnp.asarray(forward)[orient]
    to_face = jnp.asarray(backward)[orient]
    slot_pos = jnp.arange(N_ELEM * E_CAP, dtype=jnp.int32)
    live_rows = (slot_pos % E_CAP) < counts[slot_pos // E_CAP]
    face_count = face_blocks.shape[0]
    matrices = elem_mats.reshape(N_ELEM, E_CAP, 6, TRACE, 6, TRACE)
    traces = jnp.zeros(rhs.shape, jnp.float32)
    for sweep_index in range(ITERS):
        rounded = traces.astype(jnp.bfloat16)
        gathered = rounded[elem_faces]
        elem_frame = jnp.take_along_axis(gathered, to_element[:, :, None, :], axis=3)
        elem_terms = lax.map(per_device, (elem_frame.reshape(N_ELEM, E_CAP, 6, NFUN, TRACE), matrices))
        elem_terms = elem_terms.reshape(N_ELEM * E_CAP, 6, NFUN, TRACE)
        elem_terms = jnp.where(live_rows[:, None, None, None], elem_terms, jnp.zeros_like(elem_terms)).astype(jnp.bfloat16)
        face_terms = jnp.take_along_axis(elem_terms, to_face[:, :, None, :], axis=3)
        summed = jax.ops.segment_sum(face_terms.reshape(N_ELEM * E_CAP * 6, NFUN, TRACE).astype(jnp.float32), elem_faces.reshape(-1), num_segments=face_count)
        residual = (rhs.astype(jnp.float32) - summed).astype(jnp.bfloat16)
        traces = traces + jnp.einsum("fni,fij->fnj", residual.astype(jnp.float32), face_blocks.astype(jnp.float32))
    return traces
```

```python
import functools

import jax
import jax.numpy as jnp
from jax import lax
from jax.experimental import pallas as pl
from jax.experimental.pallas import tpu as pltpu
from jax.sharding import PartitionSpec as P

EDGE = 5
TRACE = 125
SLOT = 4
LIVE = 9
ZERO_ROW = 116
ROUTES = (0, 1, 3, 4)
MESH = pl.DeviceIdType.MESH


def lanes_of(values, index):
    return jnp.take_along_axis(values, index, axis=1, mode="promise_in_bounds")


def code_tables():
    shape = (48, 128)
    row = lax.broadcasted_iota(jnp.int32, shape, 0)
    lane = lax.broadcasted_iota(jnp.int32, shape, 1)
    side, code = row >> 3, row & 7

    def split(i):
        comp = (i * 1311) >> 15
        rest = i - comp * 25
        first = (rest * 205) >> 10
        return comp, first, rest - first * 5

    swap, flip_p, flip_q = (code & 4) > 0, (code & 1) > 0, (code & 2) > 0
    low = lane + 3 * side
    high = lane - (128 - 3 * side)
    node = jnp.where(low < TRACE, low, jnp.where(high >= 0, high, 0))
    comp, p, q = split(node)
    p, q = jnp.where(swap, q, p), jnp.where(swap, p, q)
    p = jnp.where(flip_p, EDGE - 1 - p, p)
    q = jnp.where(flip_q, EDGE - 1 - q, q)
    forward = comp * 25 + p * 5 + q
    comp, p, q = split(jnp.minimum(lane, TRACE - 1))
    p = jnp.where(flip_p, EDGE - 1 - p, p)
    q = jnp.where(flip_q, EDGE - 1 - q, q)
    p, q = jnp.where(swap, q, p), jnp.where(swap, p, q)
    backward = (comp * 25 + p * 5 + q + TRACE * side) & 127
    return forward, backward


def index_tables(me, devices, faces, codes, shift, count_of):
    shape = (8, 128)
    row = lax.broadcasted_iota(jnp.int32, shape, 0)
    lane = lax.broadcasted_iota(jnp.int32, shape, 1)
    packed = faces * 8 + codes
    packed = jnp.concatenate([packed, jnp.zeros((2, 256), jnp.int32)], axis=0)
    packed = pltpu.roll(packed, shift, 1)[:, :128]
    take = jnp.minimum(12 * row + (lane & 15), 127)
    flat = jnp.zeros(shape, jnp.int32)
    for k in range(6):
        source = jnp.broadcast_to(packed[k : k + 1, :], shape)
        flat = jnp.where((lane >> 4) == k, lanes_of(source, take), flat)
    face = flat >> 3
    owner = (face * 9710) >> 18
    local = face - owner * 27
    device = row + (me - 2)
    count = jnp.zeros(shape, jnp.int32)
    for r in range(5):
        count = jnp.where(row == r, count_of[r], count)
    live = (
        ((lane & 15) < count)
        & (lane < 96)
        & (row < 5)
        & (device >= 0)
        & (device < devices)
    )
    key = jnp.where(live, owner, -9)
    mine_key = jnp.broadcast_to(key[2:3, :], shape)
    mine_local = jnp.broadcast_to(local[2:3, :], shape)
    mine_code = jnp.broadcast_to(flat[2:3, :] & 7, shape)
    sends = (mine_key == device) & (row < 5)
    takes = (key == me) & (row != 2)
    both = jnp.concatenate([sends.astype(jnp.int32), takes.astype(jnp.int32)], axis=0)
    lane16 = lax.broadcasted_iota(jnp.int32, (16, 128), 1)
    rank = both
    for step in (1, 2, 4, 8, 16, 32, 64):
        rank = rank + jnp.where(lane16 >= step, pltpu.roll(rank, step, 1), 0)
    rank = rank - both
    send_rank, take_rank = rank[:8], rank[8:]
    place = jnp.where(row == 2, mine_local, 27 + SLOT * row + send_rank)
    place = jnp.sum(jnp.where(sends, place, 0), axis=0, keepdims=True)
    place = jnp.broadcast_to(place, shape)
    head = jnp.where(row == 0, place, (lane >> 4) * 8 + mine_code)
    values = jnp.concatenate([lane, local], axis=0)
    slot_of = jnp.where(both > 0, rank, -1)
    picks = jnp.zeros((16, 128), jnp.int32)
    for s in range(SLOT):
        found = jnp.sum(jnp.where(slot_of == s, values, 0), axis=1, keepdims=True)
        picks = jnp.where(lane16 == s, found, picks)
    first = jnp.concatenate([head, picks], axis=0)

    home = jnp.where(mine_key == me, local, -1)
    match = jnp.where(row == 2, home, jnp.where(takes, local, -1))
    source = jnp.where(row == 2, lane, 96 + SLOT * row + take_rank)
    tall = (32, 128)
    own = lax.broadcasted_iota(jnp.int32, tall, 0)
    lane32 = lax.broadcasted_iota(jnp.int32, tall, 1)
    most = jnp.full(tall, -1, jnp.int32)
    least = jnp.full(tall, 999, jnp.int32)
    for r in range(5):
        same = jnp.broadcast_to(match[r : r + 1, :], tall) == own
        value = jnp.broadcast_to(source[r : r + 1, :], tall)
        most = jnp.maximum(most, jnp.where(same, value, -1))
        least = jnp.minimum(least, jnp.where(same, value, 999))
    most = jnp.max(most, axis=1, keepdims=True)
    least = jnp.min(least, axis=1, keepdims=True)
    one = jnp.where(most < 0, ZERO_ROW, most)
    two = jnp.where(least >= most, ZERO_ROW, least)
    second = jnp.where(lane32 == 0, one, jnp.where(lane32 == 1, two, 0))
    return first, second


def kernel(
    devices,
    mats_hbm, blocks_hbm, rhs_hbm, faces_hbm, codes_hbm, counts_hbm,
    out_ref,
    mats, blocks, rhs, faces, codes, counts,
    first_v, second_v, first_s, second_s, forward, backward,
    table, solved, frames, terms, send_one, recv_one, send_two, recv_two,
    mat_sem, load_sem, send_sem, recv_sem,
):
    me = lax.axis_index("elem")
    start = 12 * me - 24
    base = pl.multiple_of(jnp.clip((start // 128) * 128, 0, faces_hbm.shape[1] - 256), 128)
    shift = (256 - (start - base)) % 256
    window = pl.ds(base, 256)
    loads = [
        pltpu.make_async_copy(faces_hbm.at[:, window], faces, load_sem.at[0]),
        pltpu.make_async_copy(codes_hbm.at[:, window], codes, load_sem.at[1]),
        pltpu.make_async_copy(counts_hbm, counts, load_sem.at[2]),
        pltpu.make_async_copy(rhs_hbm, rhs, load_sem.at[3]),
        pltpu.make_async_copy(blocks_hbm, blocks, load_sem.at[4]),
    ]
    for load in loads:
        load.start()
    barrier = pltpu.get_barrier_semaphore()
    peers = [lax.rem(me + (r - 2 + devices), devices) for r in range(5)]
    for r in ROUTES:
        pl.semaphore_signal(barrier, inc=1, device_id=(peers[r],), device_id_type=MESH)
    mat_loads = [
        pltpu.make_async_copy(mats_hbm.at[e], mats.at[e], mat_sem.at[e]) for e in range(LIVE)
    ]
    for load in mat_loads:
        load.start()

    table[...] = jnp.zeros_like(table)
    terms[...] = jnp.zeros_like(terms)
    forward[...], backward[...] = code_tables()

    for load in loads[:3]:
        load.wait()
    count_of = [counts[0, jnp.clip(me - 2 + r, 0, devices - 1)] for r in range(5)]
    first_v[...], second_v[...] = index_tables(
        me, devices, faces[...], codes[...], shift, count_of
    )
    tables = [
        pltpu.make_async_copy(first_v, first_s, load_sem.at[5]),
        pltpu.make_async_copy(second_v, second_s, load_sem.at[6]),
    ]
    for copy in tables:
        copy.start()

    loads[3].wait()
    loads[4].wait()
    for f in range(27):
        value = jnp.dot(rhs[f], blocks[f], preferred_element_type=jnp.float32)
        solved[f] = value
        table[f, :, :TRACE] = value.astype(jnp.bfloat16)

    for copy in tables:
        copy.wait()

    def route(send, recv, leg, r, slot):
        return pltpu.make_async_remote_copy(
            src_ref=send.at[pl.ds(SLOT * r, SLOT)],
            dst_ref=recv.at[pl.ds(SLOT * slot, SLOT)],
            send_sem=send_sem.at[leg, r],
            recv_sem=recv_sem.at[leg, slot],
            device_id=(peers[r],),
            device_id_type=MESH,
        )

    def exchange(send, recv, leg):
        for r in ROUTES:
            route(send, recv, leg, r, 4 - r).start()

    def settle(send, recv, leg):
        for r in ROUTES:
            route(send, recv, leg, r, r).wait_recv()

    for r in ROUTES:
        for s in range(SLOT):
            send_one[SLOT * r + s] = table[first_s[16 + r, s]]
    pl.semaphore_wait(barrier, 4)
    exchange(send_one, recv_one, 0)
    settle(send_one, recv_one, 0)
    for r in ROUTES:
        table[27 + SLOT * r : 27 + SLOT * (r + 1)] = recv_one[SLOT * r : SLOT * (r + 1)]

    lane = lax.broadcasted_iota(jnp.int32, (16, 128), 1)

    def gather_frame(e):
        pieces = []
        for k in range(6):
            value = table[first_s[0, k * 16 + e]].astype(jnp.float32)
            index = forward[pl.ds(first_s[1, k * 16 + e], 1), :]
            pieces.append(lanes_of(value, jnp.broadcast_to(index, (16, 128))))
        pieces.append(jnp.zeros((16, 128), jnp.float32))
        for c in range(6):
            column = jnp.where(lane < TRACE - 3 * c, pieces[c], pieces[c + 1])
            frames[e, :, 128 * c : 128 * (c + 1)] = column.astype(jnp.bfloat16)

    for e in range(LIVE):
        gather_frame(e)

    def apply(e, carry):
        pltpu.make_async_copy(mats_hbm.at[e], mats.at[e], mat_sem.at[e]).wait()
        value = jnp.dot(frames[e, :, :750], mats[e], preferred_element_type=jnp.float32)
        value = value.astype(jnp.bfloat16).astype(jnp.float32)
        value = jnp.concatenate([value, jnp.zeros((16, 18), jnp.float32)], axis=1)
        columns = [value[:, 128 * c : 128 * (c + 1)] for c in range(6)]
        for k in range(6):
            held = columns[k]
            if k:
                held = jnp.where(lane < TRACE - 3 * k, columns[k], columns[k - 1])
            index = backward[pl.ds(first_s[1, k * 16 + e], 1), :]
            moved = lanes_of(held, jnp.broadcast_to(index, (16, 128)))
            terms[k * 16 + e] = moved.astype(jnp.bfloat16)
        return carry

    lax.fori_loop(0, LIVE, apply, 0)

    for r in ROUTES:
        for s in range(SLOT):
            send_two[SLOT * r + s] = terms[first_s[8 + r, s]]
    exchange(send_two, recv_two, 1)
    settle(send_two, recv_two, 1)
    for r in ROUTES:
        terms[96 + SLOT * r : 96 + SLOT * (r + 1)] = recv_two[SLOT * r : SLOT * (r + 1)]

    for f in range(27):
        summed = terms[second_s[f, 0]].astype(jnp.float32) + terms[second_s[f, 1]].astype(
            jnp.float32
        )
        residual = (rhs[f].astype(jnp.float32) - summed[:, :TRACE]).astype(jnp.bfloat16)
        out_ref[f] = solved[f] + jnp.dot(
            residual, blocks[f], preferred_element_type=jnp.float32
        )
    for r in ROUTES:
        route(send_one, recv_one, 0, r, 4 - r).wait_send()
        route(send_two, recv_two, 1, r, 4 - r).wait_send()


def solution(mesh):
    devices = mesh.shape["elem"]

    def per_device(elem_mats, face_blocks, rhs, elem_faces, orient, counts):
        faces, functionals, trace = rhs.shape
        return pl.pallas_call(
            functools.partial(kernel, devices),
            name="sweeps",
            out_shape=jax.ShapeDtypeStruct(rhs.shape, jnp.float32),
            in_specs=[pl.BlockSpec(memory_space=pl.ANY)] * 6,
            out_specs=pl.BlockSpec(memory_space=pltpu.VMEM),
            scratch_shapes=[
                pltpu.VMEM((LIVE, 750, 750), jnp.bfloat16),
                pltpu.VMEM((faces, trace, trace), jnp.bfloat16),
                pltpu.VMEM((faces, functionals, trace), jnp.bfloat16),
                pltpu.VMEM((6, 256), jnp.int32),
                pltpu.VMEM((6, 256), jnp.int32),
                pltpu.SMEM((1, devices), jnp.int32),
                pltpu.VMEM((24, 128), jnp.int32),
                pltpu.VMEM((32, 128), jnp.int32),
                pltpu.SMEM((24, 128), jnp.int32),
                pltpu.SMEM((32, 128), jnp.int32),
                pltpu.VMEM((48, 128), jnp.int32),
                pltpu.VMEM((48, 128), jnp.int32),
                pltpu.VMEM((47, 16, 128), jnp.bfloat16),
                pltpu.VMEM((faces, functionals, trace), jnp.float32),
                pltpu.VMEM((LIVE, 16, 768), jnp.bfloat16),
                pltpu.VMEM((117, 16, 128), jnp.bfloat16),
                pltpu.VMEM((20, 16, 128), jnp.bfloat16),
                pltpu.VMEM((20, 16, 128), jnp.bfloat16),
                pltpu.VMEM((20, 16, 128), jnp.bfloat16),
                pltpu.VMEM((20, 16, 128), jnp.bfloat16),
                pltpu.SemaphoreType.DMA((LIVE,)),
                pltpu.SemaphoreType.DMA((7,)),
                pltpu.SemaphoreType.DMA((2, 5)),
                pltpu.SemaphoreType.DMA((2, 5)),
            ],
            compiler_params=pltpu.CompilerParams(collective_id=0, has_side_effects=True),
        )(elem_mats, face_blocks, rhs, elem_faces.T, orient.T, counts.reshape(1, -1))

    in_specs = (P("elem", None, None), P("elem", None, None), P("elem", None, None), P(), P(), P())
    return jax.shard_map(
        per_device, mesh=mesh, in_specs=in_specs, out_specs=P("elem", None, None), check_vma=False
    )
```

```python
import functools

import jax
import jax.numpy as jnp
from jax import lax
from jax.experimental import pallas as pl
from jax.experimental.pallas import tpu as pltpu
from jax.sharding import PartitionSpec as P

EDGE = 5
TRACE = 125
SLOT = 4
LIVE = 9
ZERO_ROW = 116
ROUTES = (0, 1, 3, 4)
MESH = pl.DeviceIdType.MESH


def lanes_of(values, index):
    return jnp.take_along_axis(values, index, axis=1, mode="promise_in_bounds")


def code_tables():
    shape = (48, 128)
    row = lax.broadcasted_iota(jnp.int32, shape, 0)
    lane = lax.broadcasted_iota(jnp.int32, shape, 1)
    side, code = row >> 3, row & 7

    def split(i):
        comp = (i * 1311) >> 15
        rest = i - comp * 25
        first = (rest * 205) >> 10
        return comp, first, rest - first * 5

    swap, flip_p, flip_q = (code & 4) > 0, (code & 1) > 0, (code & 2) > 0
    low = lane + 3 * side
    high = lane - (128 - 3 * side)
    node = jnp.where(low < TRACE, low, jnp.where(high >= 0, high, 0))
    comp, p, q = split(node)
    p, q = jnp.where(swap, q, p), jnp.where(swap, p, q)
    p = jnp.where(flip_p, EDGE - 1 - p, p)
    q = jnp.where(flip_q, EDGE - 1 - q, q)
    forward = comp * 25 + p * 5 + q
    comp, p, q = split(jnp.minimum(lane, TRACE - 1))
    p = jnp.where(flip_p, EDGE - 1 - p, p)
    q = jnp.where(flip_q, EDGE - 1 - q, q)
    p, q = jnp.where(swap, q, p), jnp.where(swap, p, q)
    backward = (comp * 25 + p * 5 + q + TRACE * side) & 127
    return forward, backward


def index_tables(me, devices, faces, codes, shift, count_of):
    shape = (8, 128)
    row = lax.broadcasted_iota(jnp.int32, shape, 0)
    lane = lax.broadcasted_iota(jnp.int32, shape, 1)
    packed = faces * 8 + codes
    packed = jnp.concatenate([packed, jnp.zeros((2, 256), jnp.int32)], axis=0)
    packed = pltpu.roll(packed, shift, 1)[:, :128]
    take = jnp.minimum(12 * row + (lane & 15), 127)
    flat = jnp.zeros(shape, jnp.int32)
    for k in range(6):
        source = jnp.broadcast_to(packed[k : k + 1, :], shape)
        flat = jnp.where((lane >> 4) == k, lanes_of(source, take), flat)
    face = flat >> 3
    owner = (face * 9710) >> 18
    local = face - owner * 27
    device = row + (me - 2)
    count = jnp.zeros(shape, jnp.int32)
    for r in range(5):
        count = jnp.where(row == r, count_of[r], count)
    live = (
        ((lane & 15) < count)
        & (lane < 96)
        & (row < 5)
        & (device >= 0)
        & (device < devices)
    )
    key = jnp.where(live, owner, -9)
    mine_key = jnp.broadcast_to(key[2:3, :], shape)
    mine_local = jnp.broadcast_to(local[2:3, :], shape)
    mine_code = jnp.broadcast_to(flat[2:3, :] & 7, shape)
    sends = (mine_key == device) & (row < 5)
    takes = (key == me) & (row != 2)
    both = jnp.concatenate([sends.astype(jnp.int32), takes.astype(jnp.int32)], axis=0)
    lane16 = lax.broadcasted_iota(jnp.int32, (16, 128), 1)
    rank = both
    for step in (1, 2, 4, 8, 16, 32, 64):
        rank = rank + jnp.where(lane16 >= step, pltpu.roll(rank, step, 1), 0)
    rank = rank - both
    send_rank, take_rank = rank[:8], rank[8:]
    place = jnp.where(row == 2, mine_local, 27 + SLOT * row + send_rank)
    place = jnp.sum(jnp.where(sends, place, 0), axis=0, keepdims=True)
    place = jnp.broadcast_to(place, shape)
    head = jnp.where(row == 0, place, (lane >> 4) * 8 + mine_code)
    values = jnp.concatenate([lane, local], axis=0)
    slot_of = jnp.where(both > 0, rank, -1)
    picks = jnp.zeros((16, 128), jnp.int32)
    for s in range(SLOT):
        found = jnp.sum(jnp.where(slot_of == s, values, 0), axis=1, keepdims=True)
        picks = jnp.where(lane16 == s, found, picks)
    first = jnp.concatenate([head, picks], axis=0)

    home = jnp.where(mine_key == me, local, -1)
    match = jnp.where(row == 2, home, jnp.where(takes, local, -1))
    source = jnp.where(row == 2, lane, 96 + SLOT * row + take_rank)
    tall = (32, 128)
    own = lax.broadcasted_iota(jnp.int32, tall, 0)
    lane32 = lax.broadcasted_iota(jnp.int32, tall, 1)
    most = jnp.full(tall, -1, jnp.int32)
    least = jnp.full(tall, 999, jnp.int32)
    for r in range(5):
        same = jnp.broadcast_to(match[r : r + 1, :], tall) == own
        value = jnp.broadcast_to(source[r : r + 1, :], tall)
        most = jnp.maximum(most, jnp.where(same, value, -1))
        least = jnp.minimum(least, jnp.where(same, value, 999))
    most = jnp.max(most, axis=1, keepdims=True)
    least = jnp.min(least, axis=1, keepdims=True)
    one = jnp.where(most < 0, ZERO_ROW, most)
    two = jnp.where(least >= most, ZERO_ROW, least)
    second = jnp.where(lane32 == 0, one, jnp.where(lane32 == 1, two, 0))
    return first, second


def kernel(
    devices,
    mats_hbm, blocks_hbm, rhs_hbm, faces_hbm, codes_hbm, counts_hbm,
    out_ref,
    mats, blocks, rhs, faces, codes, counts,
    first_v, second_v, first_s, second_s, forward, backward,
    table, solved, frames, terms, send_one, recv_one, send_two, recv_two,
    mat_sem, load_sem, send_sem, recv_sem,
):
    me = lax.axis_index("elem")
    start = 12 * me - 24
    base = pl.multiple_of(jnp.clip((start // 128) * 128, 0, faces_hbm.shape[1] - 256), 128)
    shift = (256 - (start - base)) % 256
    window = pl.ds(base, 256)
    loads = [
        pltpu.make_async_copy(faces_hbm.at[:, window], faces, load_sem.at[0]),
        pltpu.make_async_copy(codes_hbm.at[:, window], codes, load_sem.at[1]),
        pltpu.make_async_copy(counts_hbm, counts, load_sem.at[2]),
        pltpu.make_async_copy(rhs_hbm, rhs, load_sem.at[3]),
        pltpu.make_async_copy(blocks_hbm, blocks, load_sem.at[4]),
    ]
    for load in loads:
        load.start()
    barrier = pltpu.get_barrier_semaphore()
    peers = [me + (r - 2) for r in range(5)]
    exists = [(me >= 2 - r) if r < 2 else (me < devices + 2 - r) for r in range(5)]
    for r in ROUTES:

        @pl.when(exists[r])
        def _(r=r):
            pl.semaphore_signal(barrier, inc=1, device_id=(peers[r],), device_id_type=MESH)

    mat_loads = [
        pltpu.make_async_copy(mats_hbm.at[e], mats.at[e], mat_sem.at[e]) for e in range(LIVE)
    ]
    for load in mat_loads:
        load.start()

    table[...] = jnp.zeros_like(table)
    terms[...] = jnp.zeros_like(terms)
    forward[...], backward[...] = code_tables()

    for load in loads[:3]:
        load.wait()
    count_of = [counts[0, jnp.clip(me - 2 + r, 0, devices - 1)] for r in range(5)]
    first_v[...], second_v[...] = index_tables(
        me, devices, faces[...], codes[...], shift, count_of
    )
    tables = [
        pltpu.make_async_copy(first_v, first_s, load_sem.at[5]),
        pltpu.make_async_copy(second_v, second_s, load_sem.at[6]),
    ]
    for copy in tables:
        copy.start()

    loads[3].wait()
    loads[4].wait()
    for f in range(27):
        value = jnp.dot(rhs[f], blocks[f], preferred_element_type=jnp.float32)
        solved[f] = value
        table[f, :, :TRACE] = value.astype(jnp.bfloat16)

    for copy in tables:
        copy.wait()

    def route(send, recv, leg, r, slot):
        return pltpu.make_async_remote_copy(
            src_ref=send.at[pl.ds(SLOT * r, SLOT)],
            dst_ref=recv.at[pl.ds(SLOT * slot, SLOT)],
            send_sem=send_sem.at[leg, r],
            recv_sem=recv_sem.at[leg, slot],
            device_id=(peers[r],),
            device_id_type=MESH,
        )

    def exchange(send, recv, leg):
        for r in ROUTES:

            @pl.when(exists[r])
            def _(r=r):
                route(send, recv, leg, r, 4 - r).start()

    def settle(send, recv, leg):
        for r in ROUTES:

            @pl.when(exists[r])
            def _(r=r):
                route(send, recv, leg, r, r).wait_recv()

    for r in ROUTES:
        for s in range(SLOT):
            send_one[SLOT * r + s] = table[first_s[16 + r, s]]
    heard = 4 - jnp.maximum(2 - me, 0) - jnp.maximum(me - (devices - 3), 0)
    pl.semaphore_wait(barrier, heard)
    exchange(send_one, recv_one, 0)
    settle(send_one, recv_one, 0)
    for r in ROUTES:
        table[27 + SLOT * r : 27 + SLOT * (r + 1)] = recv_one[SLOT * r : SLOT * (r + 1)]

    lane = lax.broadcasted_iota(jnp.int32, (16, 128), 1)

    def gather_frame(e):
        pieces = []
        for k in range(6):
            value = table[first_s[0, k * 16 + e]].astype(jnp.float32)
            index = forward[pl.ds(first_s[1, k * 16 + e], 1), :]
            pieces.append(lanes_of(value, jnp.broadcast_to(index, (16, 128))))
        pieces.append(jnp.zeros((16, 128), jnp.float32))
        for c in range(6):
            column = jnp.where(lane < TRACE - 3 * c, pieces[c], pieces[c + 1])
            frames[e, :, 128 * c : 128 * (c + 1)] = column.astype(jnp.bfloat16)

    for e in range(LIVE):
        gather_frame(e)

    def apply(e, carry):
        pltpu.make_async_copy(mats_hbm.at[e], mats.at[e], mat_sem.at[e]).wait()
        value = jnp.dot(frames[e, :, :750], mats[e], preferred_element_type=jnp.float32)
        value = value.astype(jnp.bfloat16).astype(jnp.float32)
        value = jnp.concatenate([value, jnp.zeros((16, 18), jnp.float32)], axis=1)
        columns = [value[:, 128 * c : 128 * (c + 1)] for c in range(6)]
        for k in range(6):
            held = columns[k]
            if k:
                held = jnp.where(lane < TRACE - 3 * k, columns[k], columns[k - 1])
            index = backward[pl.ds(first_s[1, k * 16 + e], 1), :]
            moved = lanes_of(held, jnp.broadcast_to(index, (16, 128)))
            terms[k * 16 + e] = moved.astype(jnp.bfloat16)
        return carry

    lax.fori_loop(0, LIVE, apply, 0)

    for r in ROUTES:
        for s in range(SLOT):
            send_two[SLOT * r + s] = terms[first_s[8 + r, s]]
    exchange(send_two, recv_two, 1)
    settle(send_two, recv_two, 1)
    for r in ROUTES:
        terms[96 + SLOT * r : 96 + SLOT * (r + 1)] = recv_two[SLOT * r : SLOT * (r + 1)]

    for f in range(27):
        summed = terms[second_s[f, 0]].astype(jnp.float32) + terms[second_s[f, 1]].astype(
            jnp.float32
        )
        residual = (rhs[f].astype(jnp.float32) - summed[:, :TRACE]).astype(jnp.bfloat16)
        out_ref[f] = solved[f] + jnp.dot(
            residual, blocks[f], preferred_element_type=jnp.float32
        )
    for r in ROUTES:

        @pl.when(exists[r])
        def _(r=r):
            route(send_one, recv_one, 0, r, 4 - r).wait_send()
            route(send_two, recv_two, 1, r, 4 - r).wait_send()


def solution(mesh):
    devices = mesh.shape["elem"]

    def per_device(elem_mats, face_blocks, rhs, elem_faces, orient, counts):
        faces, functionals, trace = rhs.shape
        return pl.pallas_call(
            functools.partial(kernel, devices),
            name="sweeps",
            out_shape=jax.ShapeDtypeStruct(rhs.shape, jnp.float32),
            in_specs=[pl.BlockSpec(memory_space=pl.ANY)] * 6,
            out_specs=pl.BlockSpec(memory_space=pltpu.VMEM),
            scratch_shapes=[
                pltpu.VMEM((LIVE, 750, 750), jnp.bfloat16),
                pltpu.VMEM((faces, trace, trace), jnp.bfloat16),
                pltpu.VMEM((faces, functionals, trace), jnp.bfloat16),
                pltpu.VMEM((6, 256), jnp.int32),
                pltpu.VMEM((6, 256), jnp.int32),
                pltpu.SMEM((1, devices), jnp.int32),
                pltpu.VMEM((24, 128), jnp.int32),
                pltpu.VMEM((32, 128), jnp.int32),
                pltpu.SMEM((24, 128), jnp.int32),
                pltpu.SMEM((32, 128), jnp.int32),
                pltpu.VMEM((48, 128), jnp.int32),
                pltpu.VMEM((48, 128), jnp.int32),
                pltpu.VMEM((47, 16, 128), jnp.bfloat16),
                pltpu.VMEM((faces, functionals, trace), jnp.float32),
                pltpu.VMEM((LIVE, 16, 768), jnp.bfloat16),
                pltpu.VMEM((117, 16, 128), jnp.bfloat16),
                pltpu.VMEM((20, 16, 128), jnp.bfloat16),
                pltpu.VMEM((20, 16, 128), jnp.bfloat16),
                pltpu.VMEM((20, 16, 128), jnp.bfloat16),
                pltpu.VMEM((20, 16, 128), jnp.bfloat16),
                pltpu.SemaphoreType.DMA((LIVE,)),
                pltpu.SemaphoreType.DMA((7,)),
                pltpu.SemaphoreType.DMA((2, 5)),
                pltpu.SemaphoreType.DMA((2, 5)),
            ],
            compiler_params=pltpu.CompilerParams(collective_id=0, has_side_effects=True),
        )(elem_mats, face_blocks, rhs, elem_faces.T, orient.T, counts.reshape(1, -1))

    in_specs = (P("elem", None, None), P("elem", None, None), P("elem", None, None), P(), P(), P())
    return jax.shard_map(
        per_device, mesh=mesh, in_specs=in_specs, out_specs=P("elem", None, None), check_vma=False
    )
```

```python
import functools

import jax
import jax.numpy as jnp
from jax import lax
from jax.experimental import pallas as pl
from jax.experimental.pallas import tpu as pltpu
from jax.sharding import PartitionSpec as P

EDGE = 5
TRACE = 125
SLOT = 4
LIVE = 9
ZERO_ROW = 116
ROUTES = (0, 1, 3, 4)
PLANE = 32
MESH = pl.DeviceIdType.MESH


def lanes_of(values, index):
    return jnp.take_along_axis(values, index, axis=1, mode="promise_in_bounds")


def code_tables():
    shape = (48, 128)
    row = lax.broadcasted_iota(jnp.int32, shape, 0)
    lane = lax.broadcasted_iota(jnp.int32, shape, 1)
    side, code = row >> 3, row & 7

    def split(i):
        comp = (i * 1311) >> 15
        rest = i - comp * 25
        first = (rest * 205) >> 10
        return comp, first, rest - first * 5

    swap, flip_p, flip_q = (code & 4) > 0, (code & 1) > 0, (code & 2) > 0
    low = lane + 3 * side
    high = lane - (128 - 3 * side)
    node = jnp.where(low < TRACE, low, jnp.where(high >= 0, high, 0))
    comp, p, q = split(node)
    p, q = jnp.where(swap, q, p), jnp.where(swap, p, q)
    p = jnp.where(flip_p, EDGE - 1 - p, p)
    q = jnp.where(flip_q, EDGE - 1 - q, q)
    forward = comp * 25 + p * 5 + q
    comp, p, q = split(jnp.minimum(lane, TRACE - 1))
    p = jnp.where(flip_p, EDGE - 1 - p, p)
    q = jnp.where(flip_q, EDGE - 1 - q, q)
    p, q = jnp.where(swap, q, p), jnp.where(swap, p, q)
    backward = (comp * 25 + p * 5 + q + TRACE * side) & 127
    return forward, backward


def index_tables(me, devices, faces, codes, shift, count_of):
    shape = (8, 128)
    row = lax.broadcasted_iota(jnp.int32, shape, 0)
    lane = lax.broadcasted_iota(jnp.int32, shape, 1)
    packed = faces * 8 + codes
    packed = jnp.concatenate([packed, jnp.zeros((2, 256), jnp.int32)], axis=0)
    packed = pltpu.roll(packed, shift, 1)[:, :128]
    take = jnp.minimum(12 * row + (lane & 15), 127)
    flat = jnp.zeros(shape, jnp.int32)
    for k in range(6):
        source = jnp.broadcast_to(packed[k : k + 1, :], shape)
        flat = jnp.where((lane >> 4) == k, lanes_of(source, take), flat)
    face = flat >> 3
    owner = (face * 9710) >> 18
    local = face - owner * 27
    device = row + (me - 2)
    count = jnp.zeros(shape, jnp.int32)
    for r in range(5):
        count = jnp.where(row == r, count_of[r], count)
    live = (
        ((lane & 15) < count)
        & (lane < 96)
        & (row < 5)
        & (device >= 0)
        & (device < devices)
    )
    key = jnp.where(live, owner, -9)
    mine_key = jnp.broadcast_to(key[2:3, :], shape)
    mine_local = jnp.broadcast_to(local[2:3, :], shape)
    mine_code = jnp.broadcast_to(flat[2:3, :] & 7, shape)
    sends = (mine_key == device) & (row < 5)
    takes = (key == me) & (row != 2)
    both = jnp.concatenate([sends.astype(jnp.int32), takes.astype(jnp.int32)], axis=0)
    lane16 = lax.broadcasted_iota(jnp.int32, (16, 128), 1)
    rank = both
    for step in (1, 2, 4, 8, 16, 32, 64):
        rank = rank + jnp.where(lane16 >= step, pltpu.roll(rank, step, 1), 0)
    rank = rank - both
    send_rank, take_rank = rank[:8], rank[8:]
    place = jnp.where(row == 2, mine_local, 27 + SLOT * row + send_rank)
    place = jnp.sum(jnp.where(sends, place, 0), axis=0, keepdims=True)
    place = jnp.broadcast_to(place, shape)
    head = jnp.where(row == 0, place, (lane >> 4) * 8 + mine_code)
    values = jnp.concatenate([lane, local], axis=0)
    slot_of = jnp.where(both > 0, rank, -1)
    picks = jnp.zeros((16, 128), jnp.int32)
    for s in range(SLOT):
        found = jnp.sum(jnp.where(slot_of == s, values, 0), axis=1, keepdims=True)
        picks = jnp.where(lane16 == s, found, picks)
    first = jnp.concatenate([head, picks], axis=0)

    home = jnp.where(mine_key == me, local, -1)
    match = jnp.where(row == 2, home, jnp.where(takes, local, -1))
    source = jnp.where(row == 2, lane, 96 + SLOT * row + take_rank)
    tall = (32, 128)
    own = lax.broadcasted_iota(jnp.int32, tall, 0)
    lane32 = lax.broadcasted_iota(jnp.int32, tall, 1)
    most = jnp.full(tall, -1, jnp.int32)
    least = jnp.full(tall, 999, jnp.int32)
    for r in range(5):
        same = jnp.broadcast_to(match[r : r + 1, :], tall) == own
        value = jnp.broadcast_to(source[r : r + 1, :], tall)
        most = jnp.maximum(most, jnp.where(same, value, -1))
        least = jnp.minimum(least, jnp.where(same, value, 999))
    most = jnp.max(most, axis=1, keepdims=True)
    least = jnp.min(least, axis=1, keepdims=True)
    one = jnp.where(most < 0, ZERO_ROW, most)
    two = jnp.where(least >= most, ZERO_ROW, least)
    second = jnp.where(lane32 == 0, one, jnp.where(lane32 == 1, two, 0))
    return first, second


def kernel(
    devices,
    mats_hbm, blocks_hbm, rhs_hbm, faces_hbm, codes_hbm, counts_hbm,
    out_ref,
    mats, blocks, rhs, faces, codes, counts,
    first_v, second_v, first_s, second_s, forward, backward,
    table, solved, frames, terms, send_one, recv_one, send_two, recv_two,
    relay, mat_sem, load_sem, send_sem, recv_sem, relay_sem,
):
    me = lax.axis_index("elem")
    start = 12 * me - 24
    base = pl.multiple_of(jnp.clip((start // 128) * 128, 0, faces_hbm.shape[1] - 256), 128)
    shift = (256 - (start - base)) % 256
    window = pl.ds(base, 256)
    loads = [
        pltpu.make_async_copy(faces_hbm.at[:, window], faces, load_sem.at[0]),
        pltpu.make_async_copy(codes_hbm.at[:, window], codes, load_sem.at[1]),
        pltpu.make_async_copy(counts_hbm, counts, load_sem.at[2]),
        pltpu.make_async_copy(rhs_hbm, rhs, load_sem.at[3]),
        pltpu.make_async_copy(blocks_hbm, blocks, load_sem.at[4]),
    ]
    for load in loads:
        load.start()
    barrier = pltpu.get_barrier_semaphore()
    peers = [me + (r - 2) for r in range(5)]
    exists = [(me >= 2 - r) if r < 2 else (me < devices + 2 - r) for r in range(5)]
    place = lax.rem(me, PLANE)
    late = (place >= PLANE - 2) & (me < devices - PLANE)
    late_one = (place == PLANE - 1) & (me < devices - PLANE)
    early = (place < 2) & (me >= PLANE)
    early_zero = (place == 0) & (me >= PLANE)
    relays = (place >= PLANE - 8) & (place < PLANE - 6) & (me < devices - PLANE)
    relays_zero = (place == PLANE - 8) & (me < devices - PLANE)
    greets = list(exists)
    greets[3] = exists[3] & jnp.logical_not(late_one)
    greets[4] = exists[4] & jnp.logical_not(late)
    direct = list(exists)
    direct[0] = exists[0] & jnp.logical_not(early)
    direct[1] = exists[1] & jnp.logical_not(early_zero)
    signals = [(greets[r], peers[r]) for r in ROUTES]
    signals += [(late, me - 6), (late_one, me - 7), (relays, me + 8)]
    for wanted, peer in signals:

        @pl.when(wanted)
        def _(peer=peer):
            pl.semaphore_signal(barrier, inc=1, device_id=(peer,), device_id_type=MESH)

    heard = 4 - jnp.maximum(2 - me, 0) - jnp.maximum(me - (devices - 3), 0)
    heard = heard - early_zero.astype(jnp.int32)
    heard = heard + relays.astype(jnp.int32) + relays_zero.astype(jnp.int32)
    mat_loads = [
        pltpu.make_async_copy(mats_hbm.at[e], mats.at[e], mat_sem.at[e]) for e in range(LIVE)
    ]
    for load in mat_loads:
        load.start()

    table[...] = jnp.zeros_like(table)
    terms[...] = jnp.zeros_like(terms)
    forward[...], backward[...] = code_tables()

    for load in loads[:3]:
        load.wait()
    count_of = [counts[0, jnp.clip(me - 2 + r, 0, devices - 1)] for r in range(5)]
    first_v[...], second_v[...] = index_tables(
        me, devices, faces[...], codes[...], shift, count_of
    )
    tables = [
        pltpu.make_async_copy(first_v, first_s, load_sem.at[5]),
        pltpu.make_async_copy(second_v, second_s, load_sem.at[6]),
    ]
    for copy in tables:
        copy.start()

    loads[3].wait()
    loads[4].wait()
    for f in range(27):
        value = jnp.dot(rhs[f], blocks[f], preferred_element_type=jnp.float32)
        solved[f] = value
        table[f, :, :TRACE] = value.astype(jnp.bfloat16)

    for copy in tables:
        copy.wait()

    def route(send, recv, leg, r, slot):
        return pltpu.make_async_remote_copy(
            src_ref=send.at[pl.ds(SLOT * r, SLOT)],
            dst_ref=recv.at[pl.ds(SLOT * slot, SLOT)],
            send_sem=send_sem.at[leg, r],
            recv_sem=recv_sem.at[leg, slot],
            device_id=(peers[r],),
            device_id_type=MESH,
        )

    def exchange(send, recv, leg, sends):
        for r in ROUTES:

            @pl.when(sends[r])
            def _(r=r):
                route(send, recv, leg, r, 4 - r).start()

    def to_relay(r):
        return pltpu.make_async_remote_copy(
            src_ref=send_one.at[pl.ds(SLOT * r, SLOT)],
            dst_ref=relay.at[pl.ds(SLOT * r, SLOT)],
            send_sem=relay_sem.at[0, r],
            recv_sem=relay_sem.at[1, r],
            device_id=(me - 8,),
            device_id_type=MESH,
        )

    def onward(r):
        return pltpu.make_async_remote_copy(
            src_ref=relay.at[pl.ds(SLOT * r, SLOT)],
            dst_ref=recv_one.at[pl.ds(SLOT * (4 - r), SLOT)],
            send_sem=relay_sem.at[2, r],
            recv_sem=recv_sem.at[0, 4 - r],
            device_id=(me + 6 + r,),
            device_id_type=MESH,
        )

    def when_each(conditions, act):
        for r, wanted in enumerate(conditions):

            @pl.when(wanted)
            def _(r=r):
                act(r)

    def settle(send, recv, leg):
        for r in ROUTES:

            @pl.when(exists[r])
            def _(r=r):
                route(send, recv, leg, r, r).wait_recv()

    for r in ROUTES:
        for s in range(SLOT):
            send_one[SLOT * r + s] = table[first_s[16 + r, s]]
    pl.semaphore_wait(barrier, heard)
    when_each((early, early_zero), lambda r: to_relay(r).start())
    exchange(send_one, recv_one, 0, direct)

    def forward_on(r):
        to_relay(r).wait_recv()
        onward(r).start()

    when_each((relays, relays_zero), forward_on)
    settle(send_one, recv_one, 0)
    for r in ROUTES:
        table[27 + SLOT * r : 27 + SLOT * (r + 1)] = recv_one[SLOT * r : SLOT * (r + 1)]

    lane = lax.broadcasted_iota(jnp.int32, (16, 128), 1)

    def gather_frame(e):
        pieces = []
        for k in range(6):
            value = table[first_s[0, k * 16 + e]].astype(jnp.float32)
            index = forward[pl.ds(first_s[1, k * 16 + e], 1), :]
            pieces.append(lanes_of(value, jnp.broadcast_to(index, (16, 128))))
        pieces.append(jnp.zeros((16, 128), jnp.float32))
        for c in range(6):
            column = jnp.where(lane < TRACE - 3 * c, pieces[c], pieces[c + 1])
            frames[e, :, 128 * c : 128 * (c + 1)] = column.astype(jnp.bfloat16)

    for e in range(LIVE):
        gather_frame(e)

    def apply(e, carry):
        pltpu.make_async_copy(mats_hbm.at[e], mats.at[e], mat_sem.at[e]).wait()
        value = jnp.dot(frames[e, :, :750], mats[e], preferred_element_type=jnp.float32)
        value = value.astype(jnp.bfloat16).astype(jnp.float32)
        value = jnp.concatenate([value, jnp.zeros((16, 18), jnp.float32)], axis=1)
        columns = [value[:, 128 * c : 128 * (c + 1)] for c in range(6)]
        for k in range(6):
            held = columns[k]
            if k:
                held = jnp.where(lane < TRACE - 3 * k, columns[k], columns[k - 1])
            index = backward[pl.ds(first_s[1, k * 16 + e], 1), :]
            moved = lanes_of(held, jnp.broadcast_to(index, (16, 128)))
            terms[k * 16 + e] = moved.astype(jnp.bfloat16)
        return carry

    lax.fori_loop(0, LIVE, apply, 0)

    for r in ROUTES:
        for s in range(SLOT):
            send_two[SLOT * r + s] = terms[first_s[8 + r, s]]
    exchange(send_two, recv_two, 1, exists)
    settle(send_two, recv_two, 1)
    for r in ROUTES:
        terms[96 + SLOT * r : 96 + SLOT * (r + 1)] = recv_two[SLOT * r : SLOT * (r + 1)]

    for f in range(27):
        summed = terms[second_s[f, 0]].astype(jnp.float32) + terms[second_s[f, 1]].astype(
            jnp.float32
        )
        residual = (rhs[f].astype(jnp.float32) - summed[:, :TRACE]).astype(jnp.bfloat16)
        out_ref[f] = solved[f] + jnp.dot(
            residual, blocks[f], preferred_element_type=jnp.float32
        )
    when_each((early, early_zero), lambda r: to_relay(r).wait_send())
    when_each((relays, relays_zero), lambda r: onward(r).wait_send())
    for r in ROUTES:

        @pl.when(direct[r])
        def _(r=r):
            route(send_one, recv_one, 0, r, 4 - r).wait_send()

        @pl.when(exists[r])
        def _(r=r):
            route(send_two, recv_two, 1, r, 4 - r).wait_send()


def solution(mesh):
    devices = mesh.shape["elem"]

    def per_device(elem_mats, face_blocks, rhs, elem_faces, orient, counts):
        faces, functionals, trace = rhs.shape
        return pl.pallas_call(
            functools.partial(kernel, devices),
            name="sweeps",
            out_shape=pltpu.VMEM(rhs.shape, jnp.float32),
            in_specs=[pl.BlockSpec(memory_space=pl.ANY)] * 6,
            out_specs=pl.BlockSpec(memory_space=pltpu.VMEM),
            scratch_shapes=[
                pltpu.VMEM((LIVE, 750, 750), jnp.bfloat16),
                pltpu.VMEM((faces, trace, trace), jnp.bfloat16),
                pltpu.VMEM((faces, functionals, trace), jnp.bfloat16),
                pltpu.VMEM((6, 256), jnp.int32),
                pltpu.VMEM((6, 256), jnp.int32),
                pltpu.SMEM((1, devices), jnp.int32),
                pltpu.VMEM((24, 128), jnp.int32),
                pltpu.VMEM((32, 128), jnp.int32),
                pltpu.SMEM((24, 128), jnp.int32),
                pltpu.SMEM((32, 128), jnp.int32),
                pltpu.VMEM((48, 128), jnp.int32),
                pltpu.VMEM((48, 128), jnp.int32),
                pltpu.VMEM((47, 16, 128), jnp.bfloat16),
                pltpu.VMEM((faces, functionals, trace), jnp.float32),
                pltpu.VMEM((LIVE, 16, 768), jnp.bfloat16),
                pltpu.VMEM((117, 16, 128), jnp.bfloat16),
                pltpu.VMEM((20, 16, 128), jnp.bfloat16),
                pltpu.VMEM((20, 16, 128), jnp.bfloat16),
                pltpu.VMEM((20, 16, 128), jnp.bfloat16),
                pltpu.VMEM((20, 16, 128), jnp.bfloat16),
                pltpu.VMEM((8, 16, 128), jnp.bfloat16),
                pltpu.SemaphoreType.DMA((LIVE,)),
                pltpu.SemaphoreType.DMA((7,)),
                pltpu.SemaphoreType.DMA((2, 5)),
                pltpu.SemaphoreType.DMA((2, 5)),
                pltpu.SemaphoreType.DMA((3, 2)),
            ],
            compiler_params=pltpu.CompilerParams(collective_id=0, has_side_effects=True),
        )(elem_mats, face_blocks, rhs, elem_faces.T, orient.T, counts.reshape(1, -1))

    in_specs = (P("elem", None, None), P("elem", None, None), P("elem", None, None), P(), P(), P())
    return jax.shard_map(
        per_device, mesh=mesh, in_specs=in_specs, out_specs=P("elem", None, None), check_vma=False
    )
```

```python
import functools

import jax
import jax.numpy as jnp
from jax import lax
from jax.experimental import pallas as pl
from jax.experimental.pallas import tpu as pltpu
from jax.sharding import PartitionSpec as P

EDGE = 5
TRACE = 125
SLOT = 4
LIVE = 9
ARRIVED = 72
ZERO_ROW = 92
WINDOW = 142
REMOTE = 16
ROUTES = (0, 1, 3, 4)
PLANE = 32
MESH = pl.DeviceIdType.MESH


def lanes_of(values, index):
    return jnp.take_along_axis(values, index, axis=1, mode="promise_in_bounds")


def code_tables():
    shape = (48, 128)
    row = lax.broadcasted_iota(jnp.int32, shape, 0)
    lane = lax.broadcasted_iota(jnp.int32, shape, 1)
    side, code = row >> 3, row & 7

    def split(i):
        comp = (i * 1311) >> 15
        rest = i - comp * 25
        first = (rest * 205) >> 10
        return comp, first, rest - first * 5

    swap, flip_p, flip_q = (code & 4) > 0, (code & 1) > 0, (code & 2) > 0
    low = lane + 3 * side
    high = lane - (128 - 3 * side)
    node = jnp.where(low < TRACE, low, jnp.where(high >= 0, high, 0))
    comp, p, q = split(node)
    p, q = jnp.where(swap, q, p), jnp.where(swap, p, q)
    p = jnp.where(flip_p, EDGE - 1 - p, p)
    q = jnp.where(flip_q, EDGE - 1 - q, q)
    forward = comp * 25 + p * 5 + q
    comp, p, q = split(jnp.minimum(lane, TRACE - 1))
    p = jnp.where(flip_p, EDGE - 1 - p, p)
    q = jnp.where(flip_q, EDGE - 1 - q, q)
    p, q = jnp.where(swap, q, p), jnp.where(swap, p, q)
    backward = (comp * 25 + p * 5 + q + TRACE * side) & 127
    skew = row_skew(side)
    node = jnp.where(lane >= skew, lane - skew, lane + 128 - skew)
    comp, p, q = split(jnp.where(node < TRACE, node, 0))
    p, q = jnp.where(swap, q, p), jnp.where(swap, p, q)
    p = jnp.where(flip_p, EDGE - 1 - p, p)
    q = jnp.where(flip_q, EDGE - 1 - q, q)
    skewed = comp * 25 + p * 5 + q
    return forward, backward, skewed


def row_start(side):
    return jnp.where(side == 5, 608, ((TRACE * side) >> 4) << 4)


def row_skew(side):
    return TRACE * side - row_start(side)


def index_tables(me, devices, faces, codes, shift, count_of):
    shape = (8, 128)
    row = lax.broadcasted_iota(jnp.int32, shape, 0)
    lane = lax.broadcasted_iota(jnp.int32, shape, 1)
    packed = faces * 8 + codes
    packed = jnp.concatenate([packed, jnp.zeros((2, 256), jnp.int32)], axis=0)
    packed = pltpu.roll(packed, shift, 1)[:, :128]
    take = jnp.minimum(12 * row + (lane >> 3), 127)
    flat = jnp.zeros(shape, jnp.int32)
    for k in range(6):
        source = jnp.broadcast_to(packed[k : k + 1, :], shape)
        flat = jnp.where((lane & 7) == k, lanes_of(source, take), flat)
    face = flat >> 3
    owner = (face * 9710) >> 18
    local = face - owner * 27
    device = row + (me - 2)
    count = jnp.zeros(shape, jnp.int32)
    for r in range(5):
        count = jnp.where(row == r, count_of[r], count)
    live = (
        ((lane >> 3) < count)
        & ((lane & 7) < 6)
        & (row < 5)
        & (device >= 0)
        & (device < devices)
    )
    key = jnp.where(live, owner, -9)
    mine_key = jnp.broadcast_to(key[2:3, :], shape)
    mine_local = jnp.broadcast_to(local[2:3, :], shape)
    mine_code = jnp.broadcast_to(flat[2:3, :] & 7, shape)
    sends = (mine_key == device) & (row < 5)
    takes = (key == me) & (row != 2)
    sent = jnp.where(sends & (row != 2), 1, 0)
    remote = jnp.broadcast_to(jnp.sum(sent, axis=0, keepdims=True), shape)
    upper = jnp.where(row == 5, remote, jnp.where(sends, 1, 0))
    both = jnp.concatenate([upper, takes.astype(jnp.int32)], axis=0)
    lane16 = lax.broadcasted_iota(jnp.int32, (16, 128), 1)
    rank = both
    for step in (1, 2, 4, 8, 16, 32, 64):
        rank = rank + jnp.where(lane16 >= step, pltpu.roll(rank, step, 1), 0)
    rank = rank - both
    send_rank, take_rank = rank[:8], rank[8:]
    place = jnp.where(mine_key == me, mine_local, 27)
    side = lane & 7
    code = side * 8 + mine_code
    order = jnp.broadcast_to(send_rank[5:6, :], shape)
    slot = jnp.sum(jnp.where(sent > 0, SLOT * row + send_rank, 0), axis=0, keepdims=True)
    slot = jnp.broadcast_to(slot, shape)
    inner = remote
    for step in (1, 2, 4):
        inner = inner + jnp.where(side >= step, pltpu.roll(inner, step, 1), 0)
    fields = jnp.where(row == 0, slot, jnp.where(row == 1, code, lane >> 3))
    fields = jnp.where(row == 3, row_start(side) >> 4, fields)
    fields = jnp.where(row == 4, row_skew(side), fields)
    fields = jnp.where(row == 5, jnp.where(inner == remote, 0, 1), fields)
    queue = jnp.where(remote > 0, order, -1)
    listed = jnp.zeros(shape, jnp.int32)
    for q in range(REMOTE):
        found = jnp.sum(jnp.where(queue == q, fields, 0), axis=1, keepdims=True)
        listed = jnp.where(lane == q, found, listed)
    last = jnp.where((side == 7) & (inner > 0), order + remote, 0)
    for step in (1, 2, 4):
        last = last + pltpu.roll(last, 128 - step, 1)
    listed = jnp.where(row == 6, last, listed)
    head = jnp.where(row == 0, place, code)
    packed = code | ((lane >> 3) << 8) | (last << 16)
    values = jnp.concatenate([packed, local], axis=0)
    slot_of = jnp.where(both > 0, rank, -1)
    picks = jnp.zeros((16, 128), jnp.int32)
    for s in range(SLOT):
        found = jnp.sum(jnp.where(slot_of == s, values, 0), axis=1, keepdims=True)
        picks = jnp.where(lane16 == s, found, picks)
    first = jnp.concatenate([head, picks, listed], axis=0)

    home = jnp.where(mine_key == me, local, -1)
    match = jnp.where(row == 2, home, jnp.where(takes, local, -1))
    source = jnp.where(row == 2, lane, ARRIVED + SLOT * row + take_rank)
    tall = (32, 128)
    own = lax.broadcasted_iota(jnp.int32, tall, 0)
    lane32 = lax.broadcasted_iota(jnp.int32, tall, 1)
    most = jnp.full(tall, -1, jnp.int32)
    least = jnp.full(tall, 999, jnp.int32)
    for r in range(5):
        same = jnp.broadcast_to(match[r : r + 1, :], tall) == own
        value = jnp.broadcast_to(source[r : r + 1, :], tall)
        most = jnp.maximum(most, jnp.where(same, value, -1))
        least = jnp.minimum(least, jnp.where(same, value, 999))
    most = jnp.max(most, axis=1, keepdims=True)
    least = jnp.min(least, axis=1, keepdims=True)
    one = jnp.where(most < 0, ZERO_ROW, most)
    two = jnp.where(least >= most, ZERO_ROW, least)
    second = jnp.where(lane32 == 0, one, jnp.where(lane32 == 1, two, 0))
    return first, second


def kernel(
    devices,
    mats_hbm, blocks_hbm, rhs_hbm, faces_hbm, codes_hbm, counts_hbm,
    out_ref,
    mats, blocks, rhs, faces, codes, counts,
    first_v, second_v, first_s, second_s, forward, backward, skewed,
    table, solved, frames, shifted, home, sums, terms, send_one, recv_one, send_two, recv_two,
    relay, mat_sem, load_sem, send_sem, recv_sem, relay_sem,
):
    me = lax.axis_index("elem")
    start = 12 * me - 24
    base = pl.multiple_of(jnp.clip((start // 128) * 128, 0, faces_hbm.shape[1] - 256), 128)
    shift = (256 - (start - base)) % 256
    window = pl.ds(base, 256)
    loads = [
        pltpu.make_async_copy(faces_hbm.at[:, window], faces, load_sem.at[0]),
        pltpu.make_async_copy(codes_hbm.at[:, window], codes, load_sem.at[1]),
        pltpu.make_async_copy(counts_hbm, counts, load_sem.at[2]),
        pltpu.make_async_copy(rhs_hbm, rhs, load_sem.at[3]),
        pltpu.make_async_copy(blocks_hbm, blocks, load_sem.at[4]),
    ]
    for load in loads:
        load.start()
    barrier = pltpu.get_barrier_semaphore()
    peers = [me + (r - 2) for r in range(5)]
    exists = [(me >= 2 - r) if r < 2 else (me < devices + 2 - r) for r in range(5)]
    place = lax.rem(me, PLANE)
    late = (place >= PLANE - 2) & (me < devices - PLANE)
    late_one = (place == PLANE - 1) & (me < devices - PLANE)
    early = (place < 2) & (me >= PLANE)
    early_zero = (place == 0) & (me >= PLANE)
    relays = (place >= PLANE - 8) & (place < PLANE - 6) & (me < devices - PLANE)
    relays_zero = (place == PLANE - 8) & (me < devices - PLANE)
    greets = list(exists)
    greets[3] = exists[3] & jnp.logical_not(late_one)
    greets[4] = exists[4] & jnp.logical_not(late)
    direct = list(exists)
    direct[0] = exists[0] & jnp.logical_not(early)
    direct[1] = exists[1] & jnp.logical_not(early_zero)
    signals = [(greets[r], peers[r]) for r in ROUTES]
    signals += [(late, me - 6), (late_one, me - 7), (relays, me + 8)]
    for wanted, peer in signals:

        @pl.when(wanted)
        def _(peer=peer):
            pl.semaphore_signal(barrier, inc=1, device_id=(peer,), device_id_type=MESH)

    heard = 4 - jnp.maximum(2 - me, 0) - jnp.maximum(me - (devices - 3), 0)
    heard = heard - early_zero.astype(jnp.int32)
    heard = heard + relays.astype(jnp.int32) + relays_zero.astype(jnp.int32)
    mat_loads = [
        pltpu.make_async_copy(mats_hbm.at[e], mats.at[e], mat_sem.at[e]) for e in range(LIVE)
    ]
    for load in mat_loads:
        load.start()

    table[...] = jnp.zeros_like(table)
    terms[...] = jnp.zeros_like(terms)
    sums[0] = jnp.zeros_like(sums[0])
    forward[...], backward[...], skewed[...] = code_tables()

    for load in loads[:3]:
        load.wait()
    count_of = [counts[0, jnp.clip(me - 2 + r, 0, devices - 1)] for r in range(5)]
    first_v[...], second_v[...] = index_tables(
        me, devices, faces[...], codes[...], shift, count_of
    )
    tables = [
        pltpu.make_async_copy(first_v, first_s, load_sem.at[5]),
        pltpu.make_async_copy(second_v, second_s, load_sem.at[6]),
    ]
    for copy in tables:
        copy.start()

    loads[3].wait()
    loads[4].wait()
    for f in range(27):
        value = jnp.dot(rhs[f], blocks[f], preferred_element_type=jnp.float32)
        solved[f] = value
        table[f, :, :TRACE] = value.astype(jnp.bfloat16)

    for copy in tables:
        copy.wait()

    def route(send, recv, leg, r, slot):
        return pltpu.make_async_remote_copy(
            src_ref=send.at[pl.ds(SLOT * r, SLOT)],
            dst_ref=recv.at[pl.ds(SLOT * slot, SLOT)],
            send_sem=send_sem.at[leg, r],
            recv_sem=recv_sem.at[leg, slot],
            device_id=(peers[r],),
            device_id_type=MESH,
        )

    def exchange(send, recv, leg, sends):
        for r in ROUTES:

            @pl.when(sends[r])
            def _(r=r):
                route(send, recv, leg, r, 4 - r).start()

    def to_relay(r):
        return pltpu.make_async_remote_copy(
            src_ref=send_one.at[pl.ds(SLOT * r, SLOT)],
            dst_ref=relay.at[pl.ds(SLOT * r, SLOT)],
            send_sem=relay_sem.at[0, r],
            recv_sem=relay_sem.at[1, r],
            device_id=(me - 8,),
            device_id_type=MESH,
        )

    def onward(r):
        return pltpu.make_async_remote_copy(
            src_ref=relay.at[pl.ds(SLOT * r, SLOT)],
            dst_ref=recv_one.at[pl.ds(SLOT * (4 - r), SLOT)],
            send_sem=relay_sem.at[2, r],
            recv_sem=recv_sem.at[0, 4 - r],
            device_id=(me + 6 + r,),
            device_id_type=MESH,
        )

    def when_each(conditions, act):
        for r, wanted in enumerate(conditions):

            @pl.when(wanted)
            def _(r=r):
                act(r)

    def settle(send, recv, leg):
        for r in ROUTES:

            @pl.when(exists[r])
            def _(r=r):
                route(send, recv, leg, r, r).wait_recv()

    for r in ROUTES:
        for s in range(SLOT):
            send_one[SLOT * r + s] = table[first_s[16 + r, s]]
    pl.semaphore_wait(barrier, heard)
    when_each((early, early_zero), lambda r: to_relay(r).start())
    exchange(send_one, recv_one, 0, direct)

    def forward_on(r):
        to_relay(r).wait_recv()
        onward(r).start()

    lane = lax.broadcasted_iota(jnp.int32, (16, 128), 1)

    def turned(value, codes_ref, code):
        index = codes_ref[pl.ds(code, 1), :]
        return lanes_of(value, jnp.broadcast_to(index, (16, 128)))

    for e in range(LIVE):
        pieces = []
        for k in range(6):
            value = table[first_s[0, 8 * e + k]].astype(jnp.float32)
            pieces.append(turned(value, forward, first_s[1, 8 * e + k]))
        pieces.append(jnp.zeros((16, 128), jnp.float32))
        for c in range(6):
            column = jnp.where(lane < TRACE - 3 * c, pieces[c], pieces[c + 1])
            frames[e, :, 128 * c : 128 * (c + 1)] = column.astype(jnp.bfloat16)

    def columns(ref, at, value):
        for c in range(5):
            ref[at, c + 1] = value[:, 128 * c : 128 * (c + 1)]
        ref[at, 6, :, :110] = value[:, 640:750]

    def apply(e, carry):
        pltpu.make_async_copy(mats_hbm.at[e], mats.at[e], mat_sem.at[e]).wait()
        value = jnp.dot(frames[e, :, :750], mats[e], preferred_element_type=jnp.float32)
        columns(home, e, value)
        return carry

    lax.fori_loop(0, 5, apply, 0)
    when_each((relays, relays_zero), forward_on)
    lax.fori_loop(5, LIVE, apply, 0)

    settle(send_one, recv_one, 0)
    total = None
    for q in range(REMOTE):
        slot, code, e, start_row, skew, adds = [first_s[24 + i, q] for i in range(6)]
        value = turned(recv_one[slot].astype(jnp.float32), skewed, code)
        node = lane - skew
        main = jnp.where((node >= 0) & (node < TRACE), value, 0.0)
        rest = jnp.where(lane <= skew - 4, value, 0.0)
        shifted[q, :, :128] = main.astype(jnp.bfloat16)
        shifted[q, :, 128:] = rest.astype(jnp.bfloat16)
        rows = pl.ds(start_row * 16, WINDOW)
        part = jnp.dot(
            shifted[q, :, :WINDOW], mats[e, rows, :], preferred_element_type=jnp.float32
        )
        total = part if total is None else part + total * adds.astype(jnp.float32)
        columns(sums, q + 1, total)

    def term(e, k, last, code):
        value = jnp.where(
            lane < TRACE - 3 * k,
            home[e, k + 1] + sums[last, k + 1],
            home[e, k] + sums[last, k],
        )
        value = value.astype(jnp.bfloat16).astype(jnp.float32)
        return turned(value, backward, code).astype(jnp.bfloat16)

    for r in ROUTES:
        for s in range(SLOT):
            pick = first_s[8 + r, s]
            code = pick & 255
            send_two[SLOT * r + s] = term((pick >> 8) & 255, code >> 3, pick >> 16, code)
    exchange(send_two, recv_two, 1, exists)

    for e in range(LIVE):
        last = first_s[30, 8 * e]
        for k in range(6):
            terms[8 * e + k] = term(e, k, last, first_s[1, 8 * e + k])

    settle(send_two, recv_two, 1)
    for r in ROUTES:
        terms[ARRIVED + SLOT * r : ARRIVED + SLOT * (r + 1)] = recv_two[SLOT * r : SLOT * (r + 1)]

    for f in range(27):
        summed = terms[second_s[f, 0]].astype(jnp.float32) + terms[second_s[f, 1]].astype(
            jnp.float32
        )
        residual = (rhs[f].astype(jnp.float32) - summed[:, :TRACE]).astype(jnp.bfloat16)
        out_ref[f] = solved[f] + jnp.dot(
            residual, blocks[f], preferred_element_type=jnp.float32
        )
    when_each((early, early_zero), lambda r: to_relay(r).wait_send())
    when_each((relays, relays_zero), lambda r: onward(r).wait_send())
    for r in ROUTES:

        @pl.when(direct[r])
        def _(r=r):
            route(send_one, recv_one, 0, r, 4 - r).wait_send()

        @pl.when(exists[r])
        def _(r=r):
            route(send_two, recv_two, 1, r, 4 - r).wait_send()


def solution(mesh):
    devices = mesh.shape["elem"]

    def per_device(elem_mats, face_blocks, rhs, elem_faces, orient, counts):
        faces, functionals, trace = rhs.shape
        return pl.pallas_call(
            functools.partial(kernel, devices),
            name="sweeps",
            out_shape=pltpu.VMEM(rhs.shape, jnp.float32),
            in_specs=[pl.BlockSpec(memory_space=pl.ANY)] * 6,
            out_specs=pl.BlockSpec(memory_space=pltpu.VMEM),
            scratch_shapes=[
                pltpu.VMEM((LIVE, 750, 750), jnp.bfloat16),
                pltpu.VMEM((faces, trace, trace), jnp.bfloat16),
                pltpu.VMEM((faces, functionals, trace), jnp.bfloat16),
                pltpu.VMEM((6, 256), jnp.int32),
                pltpu.VMEM((6, 256), jnp.int32),
                pltpu.SMEM((1, devices), jnp.int32),
                pltpu.VMEM((32, 128), jnp.int32),
                pltpu.VMEM((32, 128), jnp.int32),
                pltpu.SMEM((32, 128), jnp.int32),
                pltpu.SMEM((32, 128), jnp.int32),
                pltpu.VMEM((48, 128), jnp.int32),
                pltpu.VMEM((48, 128), jnp.int32),
                pltpu.VMEM((48, 128), jnp.int32),
                pltpu.VMEM((28, 16, 128), jnp.bfloat16),
                pltpu.VMEM((faces, functionals, trace), jnp.float32),
                pltpu.VMEM((LIVE, 16, 768), jnp.bfloat16),
                pltpu.VMEM((REMOTE, 16, 256), jnp.bfloat16),
                pltpu.VMEM((LIVE, 7, 16, 128), jnp.float32),
                pltpu.VMEM((REMOTE + 1, 7, 16, 128), jnp.float32),
                pltpu.VMEM((ZERO_ROW + 1, 16, 128), jnp.bfloat16),
                pltpu.VMEM((20, 16, 128), jnp.bfloat16),
                pltpu.VMEM((20, 16, 128), jnp.bfloat16),
                pltpu.VMEM((20, 16, 128), jnp.bfloat16),
                pltpu.VMEM((20, 16, 128), jnp.bfloat16),
                pltpu.VMEM((8, 16, 128), jnp.bfloat16),
                pltpu.SemaphoreType.DMA((LIVE,)),
                pltpu.SemaphoreType.DMA((7,)),
                pltpu.SemaphoreType.DMA((2, 5)),
                pltpu.SemaphoreType.DMA((2, 5)),
                pltpu.SemaphoreType.DMA((3, 2)),
            ],
            compiler_params=pltpu.CompilerParams(collective_id=0, has_side_effects=True),
        )(elem_mats, face_blocks, rhs, elem_faces.T, orient.T, counts.reshape(1, -1))

    in_specs = (P("elem", None, None), P("elem", None, None), P("elem", None, None), P(), P(), P())
    return jax.shard_map(
        per_device, mesh=mesh, in_specs=in_specs, out_specs=P("elem", None, None), check_vma=False
    )
```

```python
import functools

import jax
import jax.numpy as jnp
from jax import lax
from jax.experimental import pallas as pl
from jax.experimental.pallas import tpu as pltpu
from jax.sharding import PartitionSpec as P

EDGE = 5
TRACE = 125
SLOT = 4
LIVE = 9
ARRIVED = 72
ZERO_ROW = 92
WINDOW = 142
REMOTE = 16
PICK_BACK = 80
PICK_OUT = 84
QUEUE = 88
ROUTES = (0, 1, 3, 4)
PLANE = 32
MESH = pl.DeviceIdType.MESH


def lanes_of(values, index):
    return jnp.take_along_axis(values, index, axis=1, mode="promise_in_bounds")


def code_tables():
    shape = (48, 128)
    row = lax.broadcasted_iota(jnp.int32, shape, 0)
    lane = lax.broadcasted_iota(jnp.int32, shape, 1)
    side, code = row >> 3, row & 7

    def split(i):
        comp = (i * 1311) >> 15
        rest = i - comp * 25
        first = (rest * 205) >> 10
        return comp, first, rest - first * 5

    swap, flip_p, flip_q = (code & 4) > 0, (code & 1) > 0, (code & 2) > 0
    low = lane + 3 * side
    high = lane - (128 - 3 * side)
    node = jnp.where(low < TRACE, low, jnp.where(high >= 0, high, 0))
    comp, p, q = split(node)
    p, q = jnp.where(swap, q, p), jnp.where(swap, p, q)
    p = jnp.where(flip_p, EDGE - 1 - p, p)
    q = jnp.where(flip_q, EDGE - 1 - q, q)
    forward = comp * 25 + p * 5 + q
    comp, p, q = split(jnp.minimum(lane, TRACE - 1))
    p = jnp.where(flip_p, EDGE - 1 - p, p)
    q = jnp.where(flip_q, EDGE - 1 - q, q)
    p, q = jnp.where(swap, q, p), jnp.where(swap, p, q)
    backward = (comp * 25 + p * 5 + q + TRACE * side) & 127
    skew = row_skew(side)
    node = jnp.where(lane >= skew, lane - skew, lane + 128 - skew)
    comp, p, q = split(jnp.where(node < TRACE, node, 0))
    p, q = jnp.where(swap, q, p), jnp.where(swap, p, q)
    p = jnp.where(flip_p, EDGE - 1 - p, p)
    q = jnp.where(flip_q, EDGE - 1 - q, q)
    skewed = comp * 25 + p * 5 + q
    return forward, backward, skewed


def row_start(side):
    return jnp.where(side == 5, 608, ((TRACE * side) >> 4) << 4)


def row_skew(side):
    return TRACE * side - row_start(side)


def index_tables(me, devices, right_first, faces, codes, shift, count_of):
    shape = (8, 128)
    row = lax.broadcasted_iota(jnp.int32, shape, 0)
    lane = lax.broadcasted_iota(jnp.int32, shape, 1)
    packed = faces * 8 + codes
    packed = jnp.concatenate([packed, jnp.zeros((2, 256), jnp.int32)], axis=0)
    packed = pltpu.roll(packed, shift, 1)[:, :128]
    take = jnp.minimum(12 * row + (lane >> 3), 127)
    flat = jnp.zeros(shape, jnp.int32)
    for k in range(6):
        source = jnp.broadcast_to(packed[k : k + 1, :], shape)
        flat = jnp.where((lane & 7) == k, lanes_of(source, take), flat)
    face = flat >> 3
    owner = (face * 9710) >> 18
    local = face - owner * 27
    device = row + (me - 2)
    count = jnp.zeros(shape, jnp.int32)
    for r in range(5):
        count = jnp.where(row == r, count_of[r], count)
    live = (
        ((lane >> 3) < count)
        & ((lane & 7) < 6)
        & (row < 5)
        & (device >= 0)
        & (device < devices)
    )
    key = jnp.where(live, owner, -9)
    mine_key = jnp.broadcast_to(key[2:3, :], shape)
    mine_local = jnp.broadcast_to(local[2:3, :], shape)
    mine_code = jnp.broadcast_to(flat[2:3, :] & 7, shape)
    sends = (mine_key == device) & (row < 5)
    takes = (key == me) & (row != 2)
    sent = jnp.where(sends & (row != 2), 1, 0)
    in_first = jnp.where((row > 2) == right_first, sent, 0)
    firsts = jnp.broadcast_to(jnp.sum(in_first, axis=0, keepdims=True), shape)
    remote = jnp.broadcast_to(jnp.sum(sent, axis=0, keepdims=True), shape)
    seconds = remote - firsts
    lists = jnp.where(row == 5, firsts, jnp.where(row == 6, seconds, 0))
    upper = jnp.where(row >= 5, lists, jnp.where(sends, 1, 0))
    both = jnp.concatenate([upper, takes.astype(jnp.int32)], axis=0)
    lane16 = lax.broadcasted_iota(jnp.int32, (16, 128), 1)
    rank = both
    for step in (1, 2, 4, 8, 16, 32, 64):
        rank = rank + jnp.where(lane16 >= step, pltpu.roll(rank, step, 1), 0)
    rank = rank - both
    send_rank, take_rank = rank[:8], rank[8:]
    place = jnp.where(mine_key == me, mine_local, 27)
    side = lane & 7
    code = side * 8 + mine_code
    order = jnp.where(
        firsts > 0,
        jnp.broadcast_to(send_rank[5:6, :], shape),
        REMOTE // 2 + jnp.broadcast_to(send_rank[6:7, :], shape),
    )
    base = jnp.where(row > 2, SLOT * (row - 3), SLOT * row)
    slot = jnp.sum(jnp.where(sent > 0, base + send_rank, 0), axis=0, keepdims=True)
    slot = jnp.broadcast_to(slot, shape)
    inner = lists
    for step in (1, 2, 4):
        inner = inner + jnp.where(side >= step, pltpu.roll(inner, step, 1), 0)
    earlier = jnp.where(
        firsts > 0,
        jnp.broadcast_to(inner[5:6, :], shape),
        jnp.broadcast_to(inner[6:7, :], shape),
    )
    element = lane >> 3
    adds = jnp.where(earlier == 1, 0, 1)
    field = slot | (code << 5) | (element << 11) | ((row_start(side) >> 4) << 15)
    field = field | (row_skew(side) << 21) | (adds << 26)
    queue = jnp.where(remote > 0, order, -1)
    last = jnp.where(row == 6, REMOTE // 2, 0) + send_rank
    last = jnp.where((side == 7) & (inner > 0), last, 0)
    for step in (1, 2, 4):
        last = last + pltpu.roll(last, 128 - step, 1)
    last_one = jnp.broadcast_to(last[5:6, :], shape)
    last_two = jnp.broadcast_to(last[6:7, :], shape)
    packed = code | (element << 8) | (last_one << 16) | (last_two << 24)
    first = jnp.where(row == 0, place, packed)
    values = jnp.concatenate([packed, local], axis=0)
    slot_of = jnp.where(both > 0, rank, -1)
    for s in range(SLOT):
        found = jnp.sum(jnp.where(slot_of == s, values, 0), axis=1, keepdims=True)
        first = jnp.where(lane == PICK_OUT + s, found[:8], first)
        first = jnp.where(lane == PICK_BACK + s, found[8:], first)
    for t in range(2):
        found = jnp.sum(jnp.where(queue == row + 8 * t, field, 0), axis=1, keepdims=True)
        first = jnp.where(lane == QUEUE + t, found, first)

    home = jnp.where(mine_key == me, local, -1)
    match = jnp.where(row == 2, home, jnp.where(takes, local, -1))
    source = jnp.where(row == 2, lane, ARRIVED + SLOT * row + take_rank)
    second = jnp.zeros(shape, jnp.int32)
    for t in range(4):
        own = row + 8 * t
        most = jnp.full(shape, -1, jnp.int32)
        least = jnp.full(shape, 999, jnp.int32)
        for r in range(5):
            same = jnp.broadcast_to(match[r : r + 1, :], shape) == own
            value = jnp.broadcast_to(source[r : r + 1, :], shape)
            most = jnp.maximum(most, jnp.where(same, value, -1))
            least = jnp.minimum(least, jnp.where(same, value, 999))
        most = jnp.max(most, axis=1, keepdims=True)
        least = jnp.min(least, axis=1, keepdims=True)
        one = jnp.where(most < 0, ZERO_ROW, most)
        two = jnp.where(least >= most, ZERO_ROW, least)
        second = jnp.where(lane == 2 * t, one, jnp.where(lane == 2 * t + 1, two, second))
    return first, second


def kernel(
    devices,
    mats_hbm, blocks_hbm, rhs_hbm, faces_hbm, codes_hbm, counts_hbm,
    out_ref,
    mats, blocks, rhs, faces, codes, counts,
    first_v, second_v, first_s, second_s, forward, backward, skewed,
    table, solved, frames, shifted, home, sums, terms, send_one, recv_one, send_two, recv_two,
    relay, held_one, held_two, mat_sem, load_sem, send_sem, recv_sem, relay_sem,
):
    me = lax.axis_index("elem")
    barrier = pltpu.get_barrier_semaphore()

    def greet(signals):
        for wanted, peer in signals:

            @pl.when(wanted)
            def _(peer=peer):
                pl.semaphore_signal(
                    barrier, inc=1, device_id=(peer,), device_id_type=MESH
                )

    place = lax.rem(me, PLANE)
    late = (place >= PLANE - 2) & (me < devices - PLANE)
    late_one = (place == PLANE - 1) & (me < devices - PLANE)
    early = (place < 2) & (me >= PLANE)
    early_zero = (place == 0) & (me >= PLANE)
    relays = (place >= PLANE - 8) & (place < PLANE - 6) & (me < devices - PLANE)
    relays_zero = (place == PLANE - 8) & (me < devices - PLANE)
    greet([(relays, me + 8), (late, me - 6), (late_one, me - 7)])
    start = 12 * me - 24
    base = pl.multiple_of(jnp.clip((start // 128) * 128, 0, faces_hbm.shape[1] - 256), 128)
    shift = (256 - (start - base)) % 256
    window = pl.ds(base, 256)
    loads = [
        pltpu.make_async_copy(faces_hbm.at[:, window], faces, load_sem.at[0]),
        pltpu.make_async_copy(codes_hbm.at[:, window], codes, load_sem.at[1]),
        pltpu.make_async_copy(counts_hbm, counts, load_sem.at[2]),
        pltpu.make_async_copy(rhs_hbm, rhs, load_sem.at[3]),
        pltpu.make_async_copy(blocks_hbm, blocks, load_sem.at[4]),
    ]
    for load in loads:
        load.start()
    peers = [me + (r - 2) for r in range(5)]
    exists = [(me >= 2 - r) if r < 2 else (me < devices + 2 - r) for r in range(5)]
    greets = list(exists)
    greets[3] = exists[3] & jnp.logical_not(late_one)
    greets[4] = exists[4] & jnp.logical_not(late)
    direct = list(exists)
    direct[0] = exists[0] & jnp.logical_not(early)
    direct[1] = exists[1] & jnp.logical_not(early_zero)
    right_first = lax.rem(me // 2, 4) == 0
    greet([(greets[r], peers[r]) for r in ROUTES])
    heard = 4 - jnp.maximum(2 - me, 0) - jnp.maximum(me - (devices - 3), 0)
    heard = heard - early_zero.astype(jnp.int32)
    heard = heard + relays.astype(jnp.int32) + relays_zero.astype(jnp.int32)
    mat_loads = [
        pltpu.make_async_copy(mats_hbm.at[e], mats.at[e], mat_sem.at[e]) for e in range(LIVE)
    ]

    table[...] = jnp.zeros_like(table)
    terms[...] = jnp.zeros_like(terms)
    sums[0] = jnp.zeros_like(sums[0])
    forward[...], backward[...], skewed[...] = code_tables()

    for load in loads[:3]:
        load.wait()
    for load in mat_loads:
        load.start()
    count_of = [counts[0, jnp.clip(me - 2 + r, 0, devices - 1)] for r in range(5)]
    first_v[...], second_v[...] = index_tables(
        me, devices, right_first, faces[...], codes[...], shift, count_of
    )
    tables = [
        pltpu.make_async_copy(first_v, first_s, load_sem.at[5]),
        pltpu.make_async_copy(second_v, second_s, load_sem.at[6]),
    ]
    for copy in tables:
        copy.start()

    loads[3].wait()
    loads[4].wait()
    for f in range(27):
        value = jnp.dot(rhs[f], blocks[f], preferred_element_type=jnp.float32)
        solved[f] = value
        table[f, :, :TRACE] = value.astype(jnp.bfloat16)

    for copy in tables:
        copy.wait()

    def route(send, recv, leg, r, slot):
        return pltpu.make_async_remote_copy(
            src_ref=send.at[pl.ds(SLOT * r, SLOT)],
            dst_ref=recv.at[pl.ds(SLOT * slot, SLOT)],
            send_sem=send_sem.at[leg, r],
            recv_sem=recv_sem.at[leg, slot],
            device_id=(peers[r],),
            device_id_type=MESH,
        )

    def exchange(send, recv, leg, sends):
        for r in ROUTES:

            @pl.when(sends[r])
            def _(r=r):
                route(send, recv, leg, r, 4 - r).start()

    def to_relay(r):
        return pltpu.make_async_remote_copy(
            src_ref=send_one.at[pl.ds(SLOT * r, SLOT)],
            dst_ref=relay.at[pl.ds(SLOT * r, SLOT)],
            send_sem=relay_sem.at[0, r],
            recv_sem=relay_sem.at[1, r],
            device_id=(me - 8,),
            device_id_type=MESH,
        )

    def onward(r):
        return pltpu.make_async_remote_copy(
            src_ref=relay.at[pl.ds(SLOT * r, SLOT)],
            dst_ref=recv_one.at[pl.ds(SLOT * (4 - r), SLOT)],
            send_sem=relay_sem.at[2, r],
            recv_sem=recv_sem.at[0, 4 - r],
            device_id=(me + 6 + r,),
            device_id_type=MESH,
        )

    def when_each(conditions, act):
        for r, wanted in enumerate(conditions):

            @pl.when(wanted)
            def _(r=r):
                act(r)

    def settle(send, recv, leg, routes, wanted=True):
        for r in routes:

            @pl.when(exists[r] & wanted)
            def _(r=r):
                route(send, recv, leg, r, r).wait_recv()

    for r in ROUTES:
        for s in range(SLOT):
            send_one[SLOT * r + s] = table[first_s[r, PICK_BACK + s]]
    pl.semaphore_wait(barrier, heard)
    when_each((early, early_zero), lambda r: to_relay(r).start())
    exchange(send_one, recv_one, 0, direct)

    def forward_on(r):
        to_relay(r).wait_recv()
        onward(r).start()

    lane = lax.broadcasted_iota(jnp.int32, (16, 128), 1)

    def turned(value, codes_ref, code):
        index = codes_ref[pl.ds(code, 1), :]
        return lanes_of(value, jnp.broadcast_to(index, (16, 128)))

    for e in range(LIVE):
        pieces = []
        for k in range(6):
            value = table[first_s[0, 8 * e + k]].astype(jnp.float32)
            pieces.append(turned(value, forward, first_s[1, 8 * e + k] & 255))
        pieces.append(jnp.zeros((16, 128), jnp.float32))
        for c in range(6):
            column = jnp.where(lane < TRACE - 3 * c, pieces[c], pieces[c + 1])
            frames[e, :, 128 * c : 128 * (c + 1)] = column.astype(jnp.bfloat16)

    def columns(ref, at, value):
        for c in range(5):
            ref[at, c + 1] = value[:, 128 * c : 128 * (c + 1)]
        ref[at, 6, :, :110] = value[:, 640:750]

    def apply(e, carry):
        pltpu.make_async_copy(mats_hbm.at[e], mats.at[e], mat_sem.at[e]).wait()
        value = jnp.dot(frames[e, :, :750], mats[e], preferred_element_type=jnp.float32)
        columns(home, e, value)
        return carry

    lax.fori_loop(0, 5, apply, 0)
    when_each((relays, relays_zero), forward_on)
    lax.fori_loop(5, LIVE, apply, 0)

    total = None
    for q in range(REMOTE):
        if q == 0:
            settle(send_one, recv_one, 0, (3, 4), right_first)
            settle(send_one, recv_one, 0, (0, 1), jnp.logical_not(right_first))
            held_one[...] = recv_one[pl.ds(jnp.where(right_first, 12, 0), 8)]
        if q == REMOTE // 2:
            settle(send_one, recv_one, 0, (0, 1), right_first)
            settle(send_one, recv_one, 0, (3, 4), jnp.logical_not(right_first))
            held_two[...] = recv_one[pl.ds(jnp.where(right_first, 0, 12), 8)]
            total = None
        word = first_s[q % 8, QUEUE + q // 8]
        held = held_one if q < REMOTE // 2 else held_two
        skew = (word >> 21) & 31
        value = held[word & 31].astype(jnp.float32)
        value = turned(value, skewed, (word >> 5) & 63)
        node = lane - skew
        main = jnp.where((node >= 0) & (node < TRACE), value, 0.0)
        rest = jnp.where(lane <= skew - 4, value, 0.0)
        shifted[q, :, :128] = main.astype(jnp.bfloat16)
        shifted[q, :, 128:] = rest.astype(jnp.bfloat16)
        rows = pl.ds(((word >> 15) & 63) * 16, WINDOW)
        part = jnp.dot(
            shifted[q, :, :WINDOW],
            mats[(word >> 11) & 15, rows, :],
            preferred_element_type=jnp.float32,
        )
        adds = (word >> 26).astype(jnp.float32)
        total = part if total is None else part + total * adds
        columns(sums, q + 1, total)

    def term(word):
        code, e = word & 255, (word >> 8) & 255
        one, two = (word >> 16) & 255, word >> 24
        k = code >> 3
        value = jnp.where(
            lane < TRACE - 3 * k,
            home[e, k + 1] + (sums[one, k + 1] + sums[two, k + 1]),
            home[e, k] + (sums[one, k] + sums[two, k]),
        )
        value = value.astype(jnp.bfloat16).astype(jnp.float32)
        return turned(value, backward, code).astype(jnp.bfloat16)

    for r in ROUTES:
        for s in range(SLOT):
            send_two[SLOT * r + s] = term(first_s[r, PICK_OUT + s])
    exchange(send_two, recv_two, 1, exists)

    for e in range(LIVE):
        for k in range(6):
            terms[8 * e + k] = term(first_s[1, 8 * e + k])

    settle(send_two, recv_two, 1, ROUTES)
    for r in ROUTES:
        terms[ARRIVED + SLOT * r : ARRIVED + SLOT * (r + 1)] = recv_two[SLOT * r : SLOT * (r + 1)]

    for f in range(27):
        one, two = second_s[f % 8, 2 * (f // 8)], second_s[f % 8, 2 * (f // 8) + 1]
        summed = terms[one].astype(jnp.float32) + terms[two].astype(jnp.float32)
        residual = (rhs[f].astype(jnp.float32) - summed[:, :TRACE]).astype(jnp.bfloat16)
        out_ref[f] = solved[f] + jnp.dot(
            residual, blocks[f], preferred_element_type=jnp.float32
        )
    when_each((early, early_zero), lambda r: to_relay(r).wait_send())
    when_each((relays, relays_zero), lambda r: onward(r).wait_send())
    for r in ROUTES:

        @pl.when(direct[r])
        def _(r=r):
            route(send_one, recv_one, 0, r, 4 - r).wait_send()

        @pl.when(exists[r])
        def _(r=r):
            route(send_two, recv_two, 1, r, 4 - r).wait_send()


def solution(mesh):
    devices = mesh.shape["elem"]

    def per_device(elem_mats, face_blocks, rhs, elem_faces, orient, counts):
        faces, functionals, trace = rhs.shape
        return pl.pallas_call(
            functools.partial(kernel, devices),
            name="sweeps",
            out_shape=pltpu.VMEM(rhs.shape, jnp.float32),
            in_specs=[pl.BlockSpec(memory_space=pl.ANY)] * 6,
            out_specs=pl.BlockSpec(memory_space=pltpu.VMEM),
            scratch_shapes=[
                pltpu.VMEM((LIVE, 750, 750), jnp.bfloat16),
                pltpu.VMEM((faces, trace, trace), jnp.bfloat16),
                pltpu.VMEM((faces, functionals, trace), jnp.bfloat16),
                pltpu.VMEM((6, 256), jnp.int32),
                pltpu.VMEM((6, 256), jnp.int32),
                pltpu.SMEM((1, devices), jnp.int32),
                pltpu.VMEM((8, 128), jnp.int32),
                pltpu.VMEM((8, 128), jnp.int32),
                pltpu.SMEM((8, 128), jnp.int32),
                pltpu.SMEM((8, 128), jnp.int32),
                pltpu.VMEM((48, 128), jnp.int32),
                pltpu.VMEM((48, 128), jnp.int32),
                pltpu.VMEM((48, 128), jnp.int32),
                pltpu.VMEM((28, 16, 128), jnp.bfloat16),
                pltpu.VMEM((faces, functionals, trace), jnp.float32),
                pltpu.VMEM((LIVE, 16, 768), jnp.bfloat16),
                pltpu.VMEM((REMOTE, 16, 256), jnp.bfloat16),
                pltpu.VMEM((LIVE, 7, 16, 128), jnp.float32),
                pltpu.VMEM((REMOTE + 1, 7, 16, 128), jnp.float32),
                pltpu.VMEM((ZERO_ROW + 1, 16, 128), jnp.bfloat16),
                pltpu.VMEM((20, 16, 128), jnp.bfloat16),
                pltpu.VMEM((20, 16, 128), jnp.bfloat16),
                pltpu.VMEM((20, 16, 128), jnp.bfloat16),
                pltpu.VMEM((20, 16, 128), jnp.bfloat16),
                pltpu.VMEM((8, 16, 128), jnp.bfloat16),
                pltpu.VMEM((8, 16, 128), jnp.bfloat16),
                pltpu.VMEM((8, 16, 128), jnp.bfloat16),
                pltpu.SemaphoreType.DMA((LIVE,)),
                pltpu.SemaphoreType.DMA((7,)),
                pltpu.SemaphoreType.DMA((2, 5)),
                pltpu.SemaphoreType.DMA((2, 5)),
                pltpu.SemaphoreType.DMA((3, 2)),
            ],
            compiler_params=pltpu.CompilerParams(collective_id=0, has_side_effects=True),
        )(elem_mats, face_blocks, rhs, elem_faces.T, orient.T, counts.reshape(1, -1))

    in_specs = (P("elem", None, None), P("elem", None, None), P("elem", None, None), P(), P(), P())
    return jax.shard_map(
        per_device, mesh=mesh, in_specs=in_specs, out_specs=P("elem", None, None), check_vma=False
    )
```

```python
import functools

import jax
import jax.numpy as jnp
from jax import lax
from jax.experimental import pallas as pl
from jax.experimental.pallas import tpu as pltpu
from jax.sharding import PartitionSpec as P

EDGE = 5
TRACE = 125
SLOT = 4
LIVE = 9
ARRIVED = 72
ZERO_ROW = 92
WINDOW = 142
REMOTE = 16
PICK_BACK = 80
PICK_OUT = 84
QUEUE = 88
ROUTES = (0, 1, 3, 4)
SEMS = (0, 1, None, 2, 3)
PLANE = 32
MESH = pl.DeviceIdType.MESH


def lanes_of(values, index):
    return jnp.take_along_axis(values, index, axis=1, mode="promise_in_bounds")


def code_tables():
    shape = (48, 128)
    row = lax.broadcasted_iota(jnp.int32, shape, 0)
    lane = lax.broadcasted_iota(jnp.int32, shape, 1)
    side, code = row >> 3, row & 7

    def split(i):
        comp = (i * 1311) >> 15
        rest = i - comp * 25
        first = (rest * 205) >> 10
        return comp, first, rest - first * 5

    swap, flip_p, flip_q = (code & 4) > 0, (code & 1) > 0, (code & 2) > 0
    low = lane + 3 * side
    high = lane - (128 - 3 * side)
    node = jnp.where(low < TRACE, low, jnp.where(high >= 0, high, 0))
    comp, p, q = split(node)
    p, q = jnp.where(swap, q, p), jnp.where(swap, p, q)
    p = jnp.where(flip_p, EDGE - 1 - p, p)
    q = jnp.where(flip_q, EDGE - 1 - q, q)
    forward = comp * 25 + p * 5 + q
    comp, p, q = split(jnp.minimum(lane, TRACE - 1))
    p = jnp.where(flip_p, EDGE - 1 - p, p)
    q = jnp.where(flip_q, EDGE - 1 - q, q)
    p, q = jnp.where(swap, q, p), jnp.where(swap, p, q)
    backward = (comp * 25 + p * 5 + q + TRACE * side) & 127
    skew = row_skew(side)
    node = jnp.where(lane >= skew, lane - skew, lane + 128 - skew)
    comp, p, q = split(jnp.where(node < TRACE, node, 0))
    p, q = jnp.where(swap, q, p), jnp.where(swap, p, q)
    p = jnp.where(flip_p, EDGE - 1 - p, p)
    q = jnp.where(flip_q, EDGE - 1 - q, q)
    skewed = comp * 25 + p * 5 + q
    return forward, backward, skewed


def row_start(side):
    return jnp.where(side == 5, 608, ((TRACE * side) >> 4) << 4)


def row_skew(side):
    return TRACE * side - row_start(side)


def index_tables(me, devices, right_first, faces, codes, shift, count_of):
    shape = (8, 128)
    row = lax.broadcasted_iota(jnp.int32, shape, 0)
    lane = lax.broadcasted_iota(jnp.int32, shape, 1)
    packed = faces * 8 + codes
    packed = jnp.concatenate([packed, jnp.zeros((2, 256), jnp.int32)], axis=0)
    packed = pltpu.roll(packed, shift, 1)[:, :128]
    take = jnp.minimum(12 * row + (lane >> 3), 127)
    flat = jnp.zeros(shape, jnp.int32)
    for k in range(6):
        source = jnp.broadcast_to(packed[k : k + 1, :], shape)
        flat = jnp.where((lane & 7) == k, lanes_of(source, take), flat)
    face = flat >> 3
    owner = (face * 9710) >> 18
    local = face - owner * 27
    device = row + (me - 2)
    count = jnp.zeros(shape, jnp.int32)
    for r in range(5):
        count = jnp.where(row == r, count_of[r], count)
    live = (
        ((lane >> 3) < count)
        & ((lane & 7) < 6)
        & (row < 5)
        & (device >= 0)
        & (device < devices)
    )
    key = jnp.where(live, owner, -9)
    mine_key = jnp.broadcast_to(key[2:3, :], shape)
    mine_local = jnp.broadcast_to(local[2:3, :], shape)
    mine_code = jnp.broadcast_to(flat[2:3, :] & 7, shape)
    sends = (mine_key == device) & (row < 5)
    takes = (key == me) & (row != 2)
    sent = jnp.where(sends & (row != 2), 1, 0)
    in_first = jnp.where((row > 2) == right_first, sent, 0)
    firsts = jnp.broadcast_to(jnp.sum(in_first, axis=0, keepdims=True), shape)
    remote = jnp.broadcast_to(jnp.sum(sent, axis=0, keepdims=True), shape)
    seconds = remote - firsts
    lists = jnp.where(row == 5, firsts, jnp.where(row == 6, seconds, 0))
    upper = jnp.where(row >= 5, lists, jnp.where(sends, 1, 0))
    both = jnp.concatenate([upper, takes.astype(jnp.int32)], axis=0)
    lane16 = lax.broadcasted_iota(jnp.int32, (16, 128), 1)
    rank = both
    for step in (1, 2, 4, 8, 16, 32, 64):
        rank = rank + jnp.where(lane16 >= step, pltpu.roll(rank, step, 1), 0)
    rank = rank - both
    send_rank, take_rank = rank[:8], rank[8:]
    place = jnp.where(mine_key == me, mine_local, 27)
    side = lane & 7
    code = side * 8 + mine_code
    order = jnp.where(
        firsts > 0,
        jnp.broadcast_to(send_rank[5:6, :], shape),
        REMOTE // 2 + jnp.broadcast_to(send_rank[6:7, :], shape),
    )
    base = jnp.where(row > 2, SLOT * (row - 3), SLOT * row)
    slot = jnp.sum(jnp.where(sent > 0, base + send_rank, 0), axis=0, keepdims=True)
    slot = jnp.broadcast_to(slot, shape)
    inner = lists
    for step in (1, 2, 4):
        inner = inner + jnp.where(side >= step, pltpu.roll(inner, step, 1), 0)
    earlier = jnp.where(
        firsts > 0,
        jnp.broadcast_to(inner[5:6, :], shape),
        jnp.broadcast_to(inner[6:7, :], shape),
    )
    element = lane >> 3
    adds = jnp.where(earlier == 1, 0, 1)
    field = slot | (code << 5) | (element << 11) | ((row_start(side) >> 4) << 15)
    field = field | (row_skew(side) << 21) | (adds << 26)
    queue = jnp.where(remote > 0, order, -1)
    last = jnp.where(row == 6, REMOTE // 2, 0) + send_rank
    last = jnp.where((side == 7) & (inner > 0), last, 0)
    for step in (1, 2, 4):
        last = last + pltpu.roll(last, 128 - step, 1)
    last_one = jnp.broadcast_to(last[5:6, :], shape)
    last_two = jnp.broadcast_to(last[6:7, :], shape)
    packed = code | (element << 8) | (last_one << 16) | (last_two << 24)
    first = jnp.where(row == 0, place, packed)
    values = jnp.concatenate([packed, local], axis=0)
    slot_of = jnp.where(both > 0, rank, -1)
    for s in range(SLOT):
        found = jnp.sum(jnp.where(slot_of == s, values, 0), axis=1, keepdims=True)
        first = jnp.where(lane == PICK_OUT + s, found[:8], first)
        first = jnp.where(lane == PICK_BACK + s, found[8:], first)
    for t in range(2):
        found = jnp.sum(jnp.where(queue == row + 8 * t, field, 0), axis=1, keepdims=True)
        first = jnp.where(lane == QUEUE + t, found, first)

    home = jnp.where(mine_key == me, local, -1)
    match = jnp.where(row == 2, home, jnp.where(takes, local, -1))
    source = jnp.where(row == 2, lane, ARRIVED + SLOT * row + take_rank)
    second = jnp.zeros(shape, jnp.int32)
    for t in range(4):
        own = row + 8 * t
        most = jnp.full(shape, -1, jnp.int32)
        least = jnp.full(shape, 999, jnp.int32)
        for r in range(5):
            same = jnp.broadcast_to(match[r : r + 1, :], shape) == own
            value = jnp.broadcast_to(source[r : r + 1, :], shape)
            most = jnp.maximum(most, jnp.where(same, value, -1))
            least = jnp.minimum(least, jnp.where(same, value, 999))
        most = jnp.max(most, axis=1, keepdims=True)
        least = jnp.min(least, axis=1, keepdims=True)
        one = jnp.where(most < 0, ZERO_ROW, most)
        two = jnp.where(least >= most, ZERO_ROW, least)
        second = jnp.where(lane == 2 * t, one, jnp.where(lane == 2 * t + 1, two, second))
    return first, second


def kernel(
    devices,
    mats_hbm, blocks_hbm, rhs_hbm, faces_hbm, codes_hbm, counts_hbm,
    out_ref,
    mats, blocks, rhs, faces, codes, counts,
    first_v, second_v, first_s, second_s, forward, backward, skewed,
    table, solved, frames, shifted, home, sums, terms, send_one, recv_one, send_two, recv_two,
    relay, held_one, held_two, pairs, load_sem, send_sem, recv_sem, relay_sem,
):
    me = lax.axis_index("elem")
    barrier = pltpu.get_barrier_semaphore()

    def greet(signals):
        for wanted, peer in signals:

            @pl.when(wanted)
            def _(peer=peer):
                pl.semaphore_signal(
                    barrier, inc=1, device_id=(peer,), device_id_type=MESH
                )

    place = lax.rem(me, PLANE)
    late = (place >= PLANE - 2) & (me < devices - PLANE)
    late_one = (place == PLANE - 1) & (me < devices - PLANE)
    early = (place < 2) & (me >= PLANE)
    early_zero = (place == 0) & (me >= PLANE)
    relays = (place >= PLANE - 8) & (place < PLANE - 6) & (me < devices - PLANE)
    relays_zero = (place == PLANE - 8) & (me < devices - PLANE)
    greet([(relays, me + 8), (late, me - 6), (late_one, me - 7)])
    start = 12 * me - 24
    base = pl.multiple_of(jnp.clip((start // 128) * 128, 0, faces_hbm.shape[1] - 256), 128)
    shift = (256 - (start - base)) % 256
    window = pl.ds(base, 256)
    loads = [
        pltpu.make_async_copy(faces_hbm.at[:, window], faces, load_sem.at[0]),
        pltpu.make_async_copy(codes_hbm.at[:, window], codes, load_sem.at[1]),
        pltpu.make_async_copy(counts_hbm, counts, load_sem.at[2]),
        pltpu.make_async_copy(rhs_hbm, rhs, load_sem.at[3]),
        pltpu.make_async_copy(blocks_hbm, blocks, load_sem.at[4]),
    ]
    for load in loads:
        load.start()
    peers = [me + (r - 2) for r in range(5)]
    exists = [(me >= 2 - r) if r < 2 else (me < devices + 2 - r) for r in range(5)]
    greets = list(exists)
    greets[3] = exists[3] & jnp.logical_not(late_one)
    greets[4] = exists[4] & jnp.logical_not(late)
    direct = list(exists)
    direct[0] = exists[0] & jnp.logical_not(early)
    direct[1] = exists[1] & jnp.logical_not(early_zero)
    right_first = lax.rem(me // 2, 4) == 0
    greet([(greets[r], peers[r]) for r in ROUTES])
    heard = 4 - jnp.maximum(2 - me, 0) - jnp.maximum(me - (devices - 3), 0)
    heard = heard - early_zero.astype(jnp.int32)
    heard = heard + relays.astype(jnp.int32) + relays_zero.astype(jnp.int32)
    mat_loads = [
        pltpu.make_async_copy(
            mats_hbm.at[pl.ds(3 * c, 3)], mats.at[pl.ds(3 * c, 3)], load_sem.at[c]
        )
        for c in range(3)
    ]

    table[...] = jnp.zeros_like(table)
    terms[...] = jnp.zeros_like(terms)
    pairs[...] = jnp.zeros_like(pairs)
    sums[0] = jnp.zeros_like(sums[0])
    forward[...], backward[...], skewed[...] = code_tables()

    for load in loads[:3]:
        load.wait()
    for load in mat_loads:
        load.start()
    count_of = [counts[0, jnp.clip(me - 2 + r, 0, devices - 1)] for r in range(5)]
    first_v[...], second_v[...] = index_tables(
        me, devices, right_first, faces[...], codes[...], shift, count_of
    )
    tables = [
        pltpu.make_async_copy(first_v, first_s, load_sem.at[5]),
        pltpu.make_async_copy(second_v, second_s, load_sem.at[3]),
    ]
    tables[0].start()

    loads[3].wait()
    tables[1].start()
    loads[4].wait()
    for f in range(27):
        value = jnp.dot(rhs[f], blocks[f], preferred_element_type=jnp.float32)
        solved[f] = value
        table[f, :, :TRACE] = value.astype(jnp.bfloat16)

    tables[0].wait()

    def route(send, recv, leg, r, slot):
        return pltpu.make_async_remote_copy(
            src_ref=send.at[pl.ds(SLOT * r, SLOT)],
            dst_ref=recv.at[pl.ds(SLOT * slot, SLOT)],
            send_sem=send_sem.at[SEMS[r]],
            recv_sem=recv_sem.at[leg, SEMS[slot]],
            device_id=(peers[r],),
            device_id_type=MESH,
        )

    def exchange(send, recv, leg, sends, routes=ROUTES):
        for r in routes:

            @pl.when(sends[r])
            def _(r=r):
                route(send, recv, leg, r, 4 - r).start()

    def to_relay(r):
        return pltpu.make_async_remote_copy(
            src_ref=send_one.at[pl.ds(SLOT * r, SLOT)],
            dst_ref=relay.at[pl.ds(SLOT * r, SLOT)],
            send_sem=send_sem.at[r],
            recv_sem=relay_sem.at[r],
            device_id=(me - 8,),
            device_id_type=MESH,
        )

    def onward(r):
        return pltpu.make_async_remote_copy(
            src_ref=relay.at[pl.ds(SLOT * r, SLOT)],
            dst_ref=recv_one.at[pl.ds(SLOT * (4 - r), SLOT)],
            send_sem=load_sem.at[3 + r],
            recv_sem=recv_sem.at[0, SEMS[4 - r]],
            device_id=(me + 6 + r,),
            device_id_type=MESH,
        )

    def when_each(conditions, act):
        for r, wanted in enumerate(conditions):

            @pl.when(wanted)
            def _(r=r):
                act(r)

    def settle(send, recv, leg, routes, wanted=True):
        for r in routes:

            @pl.when(exists[r] & wanted)
            def _(r=r):
                route(send, recv, leg, r, r).wait_recv()

    for r in ROUTES:
        for s in range(SLOT):
            send_one[SLOT * r + s] = table[first_s[r, PICK_BACK + s]]
    pl.semaphore_wait(barrier, heard)
    when_each((early, early_zero), lambda r: to_relay(r).start())
    exchange(send_one, recv_one, 0, direct)
    tables[1].wait()

    def forward_on(r):
        to_relay(r).wait_recv()
        onward(r).start()

    lane = lax.broadcasted_iota(jnp.int32, (16, 128), 1)

    def turned(value, codes_ref, code):
        index = codes_ref[pl.ds(code, 1), :]
        return lanes_of(value, jnp.broadcast_to(index, (16, 128)))

    for e in range(LIVE):
        pieces = []
        for k in range(6):
            value = table[first_s[0, 8 * e + k]].astype(jnp.float32)
            pieces.append(turned(value, forward, first_s[1, 8 * e + k] & 255))
        pieces.append(jnp.zeros((16, 128), jnp.float32))
        for c in range(6):
            column = jnp.where(lane < TRACE - 3 * c, pieces[c], pieces[c + 1])
            frames[e, :, 128 * c : 128 * (c + 1)] = column.astype(jnp.bfloat16)

    def columns(ref, at, value):
        for c in range(5):
            ref[at, c + 1] = value[:, 128 * c : 128 * (c + 1)]
        ref[at, 6, :, :110] = value[:, 640:750]

    def apply(e, carry):
        value = jnp.dot(frames[e, :, :750], mats[e], preferred_element_type=jnp.float32)
        columns(home, e, value)
        return carry

    mat_loads[0].wait()
    lax.fori_loop(0, 3, apply, 0)
    mat_loads[1].wait()
    lax.fori_loop(3, 4, apply, 0)
    when_each((relays, relays_zero), forward_on)
    lax.fori_loop(4, 6, apply, 0)
    mat_loads[2].wait()
    lax.fori_loop(6, LIVE, apply, 0)

    when_each((early, early_zero), lambda r: to_relay(r).wait_send())
    for r in ROUTES:

        @pl.when(direct[r])
        def _(r=r):
            route(send_one, recv_one, 0, r, 4 - r).wait_send()

    total = None
    for q in range(REMOTE):
        if q == 0:
            settle(send_one, recv_one, 0, (3, 4), right_first)
            settle(send_one, recv_one, 0, (0, 1), jnp.logical_not(right_first))
            held_one[...] = recv_one[pl.ds(jnp.where(right_first, 12, 0), 8)]
        if q == REMOTE // 2:
            settle(send_one, recv_one, 0, (0, 1), right_first)
            settle(send_one, recv_one, 0, (3, 4), jnp.logical_not(right_first))
            held_two[...] = recv_one[pl.ds(jnp.where(right_first, 0, 12), 8)]
            total = None
        word = first_s[q % 8, QUEUE + q // 8]
        held = held_one if q < REMOTE // 2 else held_two
        skew = (word >> 21) & 31
        value = held[word & 31].astype(jnp.float32)
        value = turned(value, skewed, (word >> 5) & 63)
        node = lane - skew
        main = jnp.where((node >= 0) & (node < TRACE), value, 0.0)
        rest = jnp.where(lane <= skew - 4, value, 0.0)
        shifted[q, :, :128] = main.astype(jnp.bfloat16)
        shifted[q, :, 128:] = rest.astype(jnp.bfloat16)
        rows = pl.ds(((word >> 15) & 63) * 16, WINDOW)
        part = jnp.dot(
            shifted[q, :, :WINDOW],
            mats[(word >> 11) & 15, rows, :],
            preferred_element_type=jnp.float32,
        )
        adds = (word >> 26).astype(jnp.float32)
        total = part if total is None else part + total * adds
        columns(sums, q + 1, total)

    def term(word):
        code, e = word & 255, (word >> 8) & 255
        one, two = (word >> 16) & 255, word >> 24
        k = code >> 3
        value = jnp.where(
            lane < TRACE - 3 * k,
            home[e, k + 1] + (sums[one, k + 1] + sums[two, k + 1]),
            home[e, k] + (sums[one, k] + sums[two, k]),
        )
        value = value.astype(jnp.bfloat16).astype(jnp.float32)
        return turned(value, backward, code).astype(jnp.bfloat16)

    def partials(r):
        for s in range(SLOT):
            send_two[SLOT * r + s] = term(first_s[r, PICK_OUT + s])

    for r in (4, 3, 1):
        partials(r)
    exchange(send_two, recv_two, 1, exists, (4, 3))
    partials(0)
    exchange(send_two, recv_two, 1, exists, (1, 0))

    for e in range(LIVE):
        for k in range(6):
            terms[8 * e + k] = term(first_s[1, 8 * e + k])

    for f in range(26):
        column = 128 * (f % 2)
        pairs[f // 2, :, column : column + TRACE] = blocks[f]

    settle(send_two, recv_two, 1, ROUTES)
    for r in ROUTES:
        terms[ARRIVED + SLOT * r : ARRIVED + SLOT * (r + 1)] = recv_two[SLOT * r : SLOT * (r + 1)]

    def residual(f):
        one, two = second_s[f % 8, 2 * (f // 8)], second_s[f % 8, 2 * (f // 8) + 1]
        summed = terms[one].astype(jnp.float32) + terms[two].astype(jnp.float32)
        return (rhs[f].astype(jnp.float32) - summed[:, :TRACE]).astype(jnp.bfloat16)

    for f in range(0, 26, 2):
        both = jnp.concatenate([residual(f), residual(f + 1)], axis=0)
        step = jnp.dot(both, pairs[f // 2], preferred_element_type=jnp.float32)
        out_ref[f] = solved[f] + step[:16, :TRACE]
        out_ref[f + 1] = solved[f + 1] + step[16:, 128 : 128 + TRACE]
    out_ref[26] = solved[26] + jnp.dot(
        residual(26), blocks[26], preferred_element_type=jnp.float32
    )
    when_each((relays, relays_zero), lambda r: onward(r).wait_send())
    for r in ROUTES:

        @pl.when(exists[r])
        def _(r=r):
            route(send_two, recv_two, 1, r, 4 - r).wait_send()


def solution(mesh):
    devices = mesh.shape["elem"]

    def per_device(elem_mats, face_blocks, rhs, elem_faces, orient, counts):
        faces, functionals, trace = rhs.shape
        return pl.pallas_call(
            functools.partial(kernel, devices),
            name="sweeps",
            out_shape=pltpu.VMEM(rhs.shape, jnp.float32),
            in_specs=[pl.BlockSpec(memory_space=pl.ANY)] * 6,
            out_specs=pl.BlockSpec(memory_space=pltpu.VMEM),
            scratch_shapes=[
                pltpu.VMEM((LIVE, 750, 750), jnp.bfloat16),
                pltpu.VMEM((faces, trace, trace), jnp.bfloat16),
                pltpu.VMEM((faces, functionals, trace), jnp.bfloat16),
                pltpu.VMEM((6, 256), jnp.int32),
                pltpu.VMEM((6, 256), jnp.int32),
                pltpu.SMEM((1, devices), jnp.int32),
                pltpu.VMEM((8, 128), jnp.int32),
                pltpu.VMEM((8, 128), jnp.int32),
                pltpu.SMEM((8, 128), jnp.int32),
                pltpu.SMEM((8, 128), jnp.int32),
                pltpu.VMEM((48, 128), jnp.int32),
                pltpu.VMEM((48, 128), jnp.int32),
                pltpu.VMEM((48, 128), jnp.int32),
                pltpu.VMEM((28, 16, 128), jnp.bfloat16),
                pltpu.VMEM((faces, functionals, trace), jnp.float32),
                pltpu.VMEM((LIVE, 16, 768), jnp.bfloat16),
                pltpu.VMEM((REMOTE, 16, 256), jnp.bfloat16),
                pltpu.VMEM((LIVE, 7, 16, 128), jnp.float32),
                pltpu.VMEM((REMOTE + 1, 7, 16, 128), jnp.float32),
                pltpu.VMEM((ZERO_ROW + 1, 16, 128), jnp.bfloat16),
                pltpu.VMEM((20, 16, 128), jnp.bfloat16),
                pltpu.VMEM((20, 16, 128), jnp.bfloat16),
                pltpu.VMEM((20, 16, 128), jnp.bfloat16),
                pltpu.VMEM((20, 16, 128), jnp.bfloat16),
                pltpu.VMEM((8, 16, 128), jnp.bfloat16),
                pltpu.VMEM((8, 16, 128), jnp.bfloat16),
                pltpu.VMEM((8, 16, 128), jnp.bfloat16),
                pltpu.VMEM((13, trace, 256), jnp.bfloat16),
                pltpu.SemaphoreType.DMA((6,)),
                pltpu.SemaphoreType.DMA((4,)),
                pltpu.SemaphoreType.DMA((2, 4)),
                pltpu.SemaphoreType.DMA((2,)),
            ],
            compiler_params=pltpu.CompilerParams(collective_id=0, has_side_effects=True),
        )(elem_mats, face_blocks, rhs, elem_faces.T, orient.T, counts.reshape(1, -1))

    in_specs = (P("elem", None, None), P("elem", None, None), P("elem", None, None), P(), P(), P())
    return jax.shard_map(
        per_device, mesh=mesh, in_specs=in_specs, out_specs=P("elem", None, None), check_vma=False
    )
```

```python
import functools

import jax
import jax.numpy as jnp
from jax import lax
from jax.experimental import pallas as pl
from jax.experimental.pallas import tpu as pltpu
from jax.sharding import PartitionSpec as P

EDGE = 5
TRACE = 125
SLOT = 4
LIVE = 9
ARRIVED = 72
ZERO_ROW = 92
WINDOW = 142
REMOTE = 16
PICK_BACK = 80
PICK_OUT = 84
QUEUE = 88
ROUTES = (0, 1, 3, 4)
SEMS = (0, 1, None, 2, 3)
PLANE = 32
MESH = pl.DeviceIdType.MESH


def lanes_of(values, index):
    return jnp.take_along_axis(values, index, axis=1, mode="promise_in_bounds")


def code_tables():
    shape = (48, 128)
    row = lax.broadcasted_iota(jnp.int32, shape, 0)
    lane = lax.broadcasted_iota(jnp.int32, shape, 1)
    side, code = row >> 3, row & 7

    def split(i):
        comp = (i * 1311) >> 15
        rest = i - comp * 25
        first = (rest * 205) >> 10
        return comp, first, rest - first * 5

    swap, flip_p, flip_q = (code & 4) > 0, (code & 1) > 0, (code & 2) > 0
    low = lane + 3 * side
    high = lane - (128 - 3 * side)
    node = jnp.where(low < TRACE, low, jnp.where(high >= 0, high, 0))
    comp, p, q = split(node)
    p, q = jnp.where(swap, q, p), jnp.where(swap, p, q)
    p = jnp.where(flip_p, EDGE - 1 - p, p)
    q = jnp.where(flip_q, EDGE - 1 - q, q)
    forward = comp * 25 + p * 5 + q
    comp, p, q = split(jnp.minimum(lane, TRACE - 1))
    p = jnp.where(flip_p, EDGE - 1 - p, p)
    q = jnp.where(flip_q, EDGE - 1 - q, q)
    p, q = jnp.where(swap, q, p), jnp.where(swap, p, q)
    backward = (comp * 25 + p * 5 + q + TRACE * side) & 127
    skew = row_skew(side)
    node = jnp.where(lane >= skew, lane - skew, lane + 128 - skew)
    comp, p, q = split(jnp.where(node < TRACE, node, 0))
    p, q = jnp.where(swap, q, p), jnp.where(swap, p, q)
    p = jnp.where(flip_p, EDGE - 1 - p, p)
    q = jnp.where(flip_q, EDGE - 1 - q, q)
    skewed = comp * 25 + p * 5 + q
    return forward, backward, skewed


def row_start(side):
    return jnp.where(side == 5, 608, ((TRACE * side) >> 4) << 4)


def row_skew(side):
    return TRACE * side - row_start(side)


def index_tables(me, devices, right_first, faces, codes, shift, count_of):
    shape = (8, 128)
    row = lax.broadcasted_iota(jnp.int32, shape, 0)
    lane = lax.broadcasted_iota(jnp.int32, shape, 1)
    packed = faces * 8 + codes
    packed = jnp.concatenate([packed, jnp.zeros((2, 256), jnp.int32)], axis=0)
    packed = pltpu.roll(packed, shift, 1)[:, :128]
    take = jnp.minimum(12 * row + (lane >> 3), 127)
    flat = jnp.zeros(shape, jnp.int32)
    for k in range(6):
        source = jnp.broadcast_to(packed[k : k + 1, :], shape)
        flat = jnp.where((lane & 7) == k, lanes_of(source, take), flat)
    face = flat >> 3
    owner = (face * 9710) >> 18
    local = face - owner * 27
    device = row + (me - 2)
    count = jnp.zeros(shape, jnp.int32)
    for r in range(5):
        count = jnp.where(row == r, count_of[r], count)
    live = (
        ((lane >> 3) < count)
        & ((lane & 7) < 6)
        & (row < 5)
        & (device >= 0)
        & (device < devices)
    )
    key = jnp.where(live, owner, -9)
    mine_key = jnp.broadcast_to(key[2:3, :], shape)
    mine_local = jnp.broadcast_to(local[2:3, :], shape)
    mine_code = jnp.broadcast_to(flat[2:3, :] & 7, shape)
    sends = (mine_key == device) & (row < 5)
    takes = (key == me) & (row != 2)
    sent = jnp.where(sends & (row != 2), 1, 0)
    in_first = jnp.where((row > 2) == right_first, sent, 0)
    firsts = jnp.broadcast_to(jnp.sum(in_first, axis=0, keepdims=True), shape)
    remote = jnp.broadcast_to(jnp.sum(sent, axis=0, keepdims=True), shape)
    seconds = remote - firsts
    lists = jnp.where(row == 5, firsts, jnp.where(row == 6, seconds, 0))
    upper = jnp.where(row >= 5, lists, jnp.where(sends, 1, 0))
    both = jnp.concatenate([upper, takes.astype(jnp.int32)], axis=0)
    lane16 = lax.broadcasted_iota(jnp.int32, (16, 128), 1)
    rank = both
    for step in (1, 2, 4, 8, 16, 32, 64):
        rank = rank + jnp.where(lane16 >= step, pltpu.roll(rank, step, 1), 0)
    rank = rank - both
    send_rank, take_rank = rank[:8], rank[8:]
    place = jnp.where(mine_key == me, mine_local, 27)
    side = lane & 7
    code = side * 8 + mine_code
    order = jnp.where(
        firsts > 0,
        jnp.broadcast_to(send_rank[5:6, :], shape),
        REMOTE // 2 + jnp.broadcast_to(send_rank[6:7, :], shape),
    )
    base = jnp.where(row > 2, SLOT * (row - 3), SLOT * row)
    slot = jnp.sum(jnp.where(sent > 0, base + send_rank, 0), axis=0, keepdims=True)
    slot = jnp.broadcast_to(slot, shape)
    inner = lists
    for step in (1, 2, 4):
        inner = inner + jnp.where(side >= step, pltpu.roll(inner, step, 1), 0)
    earlier = jnp.where(
        firsts > 0,
        jnp.broadcast_to(inner[5:6, :], shape),
        jnp.broadcast_to(inner[6:7, :], shape),
    )
    element = lane >> 3
    adds = jnp.where(earlier == 1, 0, 1)
    field = slot | (code << 5) | (element << 11) | ((row_start(side) >> 4) << 15)
    field = field | (row_skew(side) << 21) | (adds << 26)
    queue = jnp.where(remote > 0, order, -1)
    last = jnp.where(row == 6, REMOTE // 2, 0) + send_rank
    last = jnp.where((side == 7) & (inner > 0), last, 0)
    for step in (1, 2, 4):
        last = last + pltpu.roll(last, 128 - step, 1)
    last_one = jnp.broadcast_to(last[5:6, :], shape)
    last_two = jnp.broadcast_to(last[6:7, :], shape)
    packed = code | (element << 8) | (last_one << 16) | (last_two << 24)
    first = jnp.where(row == 0, place, packed)
    values = jnp.concatenate([packed, local], axis=0)
    slot_of = jnp.where(both > 0, rank, -1)
    for s in range(SLOT):
        found = jnp.sum(jnp.where(slot_of == s, values, 0), axis=1, keepdims=True)
        first = jnp.where(lane == PICK_OUT + s, found[:8], first)
        first = jnp.where(lane == PICK_BACK + s, found[8:], first)
    for t in range(2):
        found = jnp.sum(jnp.where(queue == row + 8 * t, field, 0), axis=1, keepdims=True)
        first = jnp.where(lane == QUEUE + t, found, first)

    home = jnp.where(mine_key == me, local, -1)
    match = jnp.where(row == 2, home, jnp.where(takes, local, -1))
    source = jnp.where(row == 2, lane, ARRIVED + SLOT * row + take_rank)
    second = jnp.zeros(shape, jnp.int32)
    for t in range(4):
        own = row + 8 * t
        most = jnp.full(shape, -1, jnp.int32)
        least = jnp.full(shape, 999, jnp.int32)
        for r in range(5):
            same = jnp.broadcast_to(match[r : r + 1, :], shape) == own
            value = jnp.broadcast_to(source[r : r + 1, :], shape)
            most = jnp.maximum(most, jnp.where(same, value, -1))
            least = jnp.minimum(least, jnp.where(same, value, 999))
        most = jnp.max(most, axis=1, keepdims=True)
        least = jnp.min(least, axis=1, keepdims=True)
        one = jnp.where(most < 0, ZERO_ROW, most)
        two = jnp.where(least >= most, ZERO_ROW, least)
        second = jnp.where(lane == 2 * t, one, jnp.where(lane == 2 * t + 1, two, second))
    return first, second


def kernel(
    devices,
    mats_hbm, blocks_hbm, rhs_hbm, faces_hbm, codes_hbm, counts_hbm,
    out_ref,
    mats, blocks, rhs, faces, codes, counts,
    first_v, second_v, first_s, second_s, forward, backward, skewed,
    table, solved, frames, shifted, home, sums, terms, send_one, recv_one, send_two, recv_two,
    relay, held_one, held_two, pairs, load_sem, send_sem, recv_sem, relay_sem,
):
    me = lax.axis_index("elem")
    barrier = pltpu.get_barrier_semaphore()

    def greet(signals):
        for wanted, peer in signals:

            @pl.when(wanted)
            def _(peer=peer):
                pl.semaphore_signal(
                    barrier, inc=1, device_id=(peer,), device_id_type=MESH
                )

    place = lax.rem(me, PLANE)
    late = (place >= PLANE - 2) & (me < devices - PLANE)
    late_one = (place == PLANE - 1) & (me < devices - PLANE)
    early = (place < 2) & (me >= PLANE)
    early_zero = (place == 0) & (me >= PLANE)
    relays = (place >= PLANE - 8) & (place < PLANE - 6) & (me >= PLANE)
    relays_zero = (place == PLANE - 8) & (me >= PLANE)
    greet([(relays, me - 24), (late, me + 26), (late_one, me + 25)])
    start = 12 * me - 24
    base = pl.multiple_of(jnp.clip((start // 128) * 128, 0, faces_hbm.shape[1] - 256), 128)
    shift = (256 - (start - base)) % 256
    window = pl.ds(base, 256)
    loads = [
        pltpu.make_async_copy(faces_hbm.at[:, window], faces, load_sem.at[0]),
        pltpu.make_async_copy(codes_hbm.at[:, window], codes, load_sem.at[1]),
        pltpu.make_async_copy(counts_hbm, counts, load_sem.at[2]),
        pltpu.make_async_copy(rhs_hbm, rhs, load_sem.at[3]),
        pltpu.make_async_copy(blocks_hbm, blocks, load_sem.at[4]),
    ]
    for load in loads:
        load.start()
    peers = [me + (r - 2) for r in range(5)]
    exists = [(me >= 2 - r) if r < 2 else (me < devices + 2 - r) for r in range(5)]
    greets = list(exists)
    greets[3] = exists[3] & jnp.logical_not(late_one)
    greets[4] = exists[4] & jnp.logical_not(late)
    direct = list(exists)
    direct[0] = exists[0] & jnp.logical_not(early)
    direct[1] = exists[1] & jnp.logical_not(early_zero)
    right_first = lax.rem(me // 2, 4) == 0
    greet([(greets[r], peers[r]) for r in ROUTES])
    heard = 4 - jnp.maximum(2 - me, 0) - jnp.maximum(me - (devices - 3), 0)
    heard = heard - early_zero.astype(jnp.int32)
    heard = heard + relays.astype(jnp.int32) + relays_zero.astype(jnp.int32)
    mat_loads = [
        pltpu.make_async_copy(
            mats_hbm.at[pl.ds(3 * c, 3)], mats.at[pl.ds(3 * c, 3)], load_sem.at[c]
        )
        for c in range(3)
    ]

    table[...] = jnp.zeros_like(table)
    terms[...] = jnp.zeros_like(terms)
    pairs[...] = jnp.zeros_like(pairs)
    sums[0] = jnp.zeros_like(sums[0])
    forward[...], backward[...], skewed[...] = code_tables()

    for load in loads[:3]:
        load.wait()
    for load in mat_loads:
        load.start()
    count_of = [counts[0, jnp.clip(me - 2 + r, 0, devices - 1)] for r in range(5)]
    first_v[...], second_v[...] = index_tables(
        me, devices, right_first, faces[...], codes[...], shift, count_of
    )
    tables = [
        pltpu.make_async_copy(first_v, first_s, load_sem.at[5]),
        pltpu.make_async_copy(second_v, second_s, load_sem.at[3]),
    ]
    tables[0].start()

    loads[3].wait()
    tables[1].start()
    loads[4].wait()
    for f in range(27):
        value = jnp.dot(rhs[f], blocks[f], preferred_element_type=jnp.float32)
        solved[f] = value
        table[f, :, :TRACE] = value.astype(jnp.bfloat16)

    tables[0].wait()

    def route(send, recv, leg, r, slot):
        return pltpu.make_async_remote_copy(
            src_ref=send.at[pl.ds(SLOT * r, SLOT)],
            dst_ref=recv.at[pl.ds(SLOT * slot, SLOT)],
            send_sem=send_sem.at[SEMS[r]],
            recv_sem=recv_sem.at[leg, SEMS[slot]],
            device_id=(peers[r],),
            device_id_type=MESH,
        )

    def exchange(send, recv, leg, sends, routes=ROUTES):
        for r in routes:

            @pl.when(sends[r])
            def _(r=r):
                route(send, recv, leg, r, 4 - r).start()

    def to_relay(r):
        return pltpu.make_async_remote_copy(
            src_ref=send_one.at[pl.ds(SLOT * r, SLOT)],
            dst_ref=relay.at[pl.ds(SLOT * r, SLOT)],
            send_sem=send_sem.at[r],
            recv_sem=relay_sem.at[r],
            device_id=(me + 24,),
            device_id_type=MESH,
        )

    def onward(r):
        return pltpu.make_async_remote_copy(
            src_ref=relay.at[pl.ds(SLOT * r, SLOT)],
            dst_ref=recv_one.at[pl.ds(SLOT * (4 - r), SLOT)],
            send_sem=load_sem.at[3 + r],
            recv_sem=recv_sem.at[0, SEMS[4 - r]],
            device_id=(me - 26 + r,),
            device_id_type=MESH,
        )

    def when_each(conditions, act):
        for r, wanted in enumerate(conditions):

            @pl.when(wanted)
            def _(r=r):
                act(r)

    def settle(send, recv, leg, routes, wanted=True):
        for r in routes:

            @pl.when(exists[r] & wanted)
            def _(r=r):
                route(send, recv, leg, r, r).wait_recv()

    for r in ROUTES:
        for s in range(SLOT):
            send_one[SLOT * r + s] = table[first_s[r, PICK_BACK + s]]
    pl.semaphore_wait(barrier, heard)
    when_each((early, early_zero), lambda r: to_relay(r).start())
    exchange(send_one, recv_one, 0, direct)
    tables[1].wait()

    def forward_on(r):
        to_relay(r).wait_recv()
        onward(r).start()

    lane = lax.broadcasted_iota(jnp.int32, (16, 128), 1)

    def turned(value, codes_ref, code):
        index = codes_ref[pl.ds(code, 1), :]
        return lanes_of(value, jnp.broadcast_to(index, (16, 128)))

    for e in range(LIVE):
        pieces = []
        for k in range(6):
            value = table[first_s[0, 8 * e + k]].astype(jnp.float32)
            pieces.append(turned(value, forward, first_s[1, 8 * e + k] & 255))
        pieces.append(jnp.zeros((16, 128), jnp.float32))
        for c in range(6):
            column = jnp.where(lane < TRACE - 3 * c, pieces[c], pieces[c + 1])
            frames[e, :, 128 * c : 128 * (c + 1)] = column.astype(jnp.bfloat16)

    def columns(ref, at, value):
        for c in range(5):
            ref[at, c + 1] = value[:, 128 * c : 128 * (c + 1)]
        ref[at, 6, :, :110] = value[:, 640:750]

    def apply(e, carry):
        value = jnp.dot(frames[e, :, :750], mats[e], preferred_element_type=jnp.float32)
        columns(home, e, value)
        return carry

    when_each((relays, relays_zero), forward_on)
    mat_loads[0].wait()
    lax.fori_loop(0, 3, apply, 0)
    mat_loads[1].wait()
    lax.fori_loop(3, 4, apply, 0)
    lax.fori_loop(4, 6, apply, 0)
    mat_loads[2].wait()
    lax.fori_loop(6, LIVE, apply, 0)

    when_each((early, early_zero), lambda r: to_relay(r).wait_send())
    for r in ROUTES:

        @pl.when(direct[r])
        def _(r=r):
            route(send_one, recv_one, 0, r, 4 - r).wait_send()

    total = None
    for q in range(REMOTE):
        if q == 0:
            settle(send_one, recv_one, 0, (3, 4), right_first)
            settle(send_one, recv_one, 0, (0, 1), jnp.logical_not(right_first))
            held_one[...] = recv_one[pl.ds(jnp.where(right_first, 12, 0), 8)]
        if q == REMOTE // 2:
            settle(send_one, recv_one, 0, (0, 1), right_first)
            settle(send_one, recv_one, 0, (3, 4), jnp.logical_not(right_first))
            held_two[...] = recv_one[pl.ds(jnp.where(right_first, 0, 12), 8)]
            total = None
        word = first_s[q % 8, QUEUE + q // 8]
        held = held_one if q < REMOTE // 2 else held_two
        skew = (word >> 21) & 31
        value = held[word & 31].astype(jnp.float32)
        value = turned(value, skewed, (word >> 5) & 63)
        node = lane - skew
        main = jnp.where((node >= 0) & (node < TRACE), value, 0.0)
        rest = jnp.where(lane <= skew - 4, value, 0.0)
        shifted[q, :, :128] = main.astype(jnp.bfloat16)
        shifted[q, :, 128:] = rest.astype(jnp.bfloat16)
        rows = pl.ds(((word >> 15) & 63) * 16, WINDOW)
        part = jnp.dot(
            shifted[q, :, :WINDOW],
            mats[(word >> 11) & 15, rows, :],
            preferred_element_type=jnp.float32,
        )
        adds = (word >> 26).astype(jnp.float32)
        total = part if total is None else part + total * adds
        columns(sums, q + 1, total)

    def term(word):
        code, e = word & 255, (word >> 8) & 255
        one, two = (word >> 16) & 255, word >> 24
        k = code >> 3
        value = jnp.where(
            lane < TRACE - 3 * k,
            home[e, k + 1] + (sums[one, k + 1] + sums[two, k + 1]),
            home[e, k] + (sums[one, k] + sums[two, k]),
        )
        value = value.astype(jnp.bfloat16).astype(jnp.float32)
        return turned(value, backward, code).astype(jnp.bfloat16)

    def partials(r):
        for s in range(SLOT):
            send_two[SLOT * r + s] = term(first_s[r, PICK_OUT + s])

    for r in (4, 3, 1):
        partials(r)
    exchange(send_two, recv_two, 1, exists, (4, 3))
    partials(0)
    exchange(send_two, recv_two, 1, exists, (1, 0))

    for e in range(LIVE):
        for k in range(6):
            terms[8 * e + k] = term(first_s[1, 8 * e + k])

    for f in range(26):
        column = 128 * (f % 2)
        pairs[f // 2, :, column : column + TRACE] = blocks[f]

    settle(send_two, recv_two, 1, ROUTES)
    for r in ROUTES:
        terms[ARRIVED + SLOT * r : ARRIVED + SLOT * (r + 1)] = recv_two[SLOT * r : SLOT * (r + 1)]

    def residual(f):
        one, two = second_s[f % 8, 2 * (f // 8)], second_s[f % 8, 2 * (f // 8) + 1]
        summed = terms[one].astype(jnp.float32) + terms[two].astype(jnp.float32)
        return (rhs[f].astype(jnp.float32) - summed[:, :TRACE]).astype(jnp.bfloat16)

    for f in range(0, 26, 2):
        both = jnp.concatenate([residual(f), residual(f + 1)], axis=0)
        step = jnp.dot(both, pairs[f // 2], preferred_element_type=jnp.float32)
        out_ref[f] = solved[f] + step[:16, :TRACE]
        out_ref[f + 1] = solved[f + 1] + step[16:, 128 : 128 + TRACE]
    out_ref[26] = solved[26] + jnp.dot(
        residual(26), blocks[26], preferred_element_type=jnp.float32
    )
    when_each((relays, relays_zero), lambda r: onward(r).wait_send())
    for r in ROUTES:

        @pl.when(exists[r])
        def _(r=r):
            route(send_two, recv_two, 1, r, 4 - r).wait_send()


def solution(mesh):
    devices = mesh.shape["elem"]

    def per_device(elem_mats, face_blocks, rhs, elem_faces, orient, counts):
        faces, functionals, trace = rhs.shape
        return pl.pallas_call(
            functools.partial(kernel, devices),
            name="sweeps",
            out_shape=pltpu.VMEM(rhs.shape, jnp.float32),
            in_specs=[pl.BlockSpec(memory_space=pl.ANY)] * 6,
            out_specs=pl.BlockSpec(memory_space=pltpu.VMEM),
            scratch_shapes=[
                pltpu.VMEM((LIVE, 750, 750), jnp.bfloat16),
                pltpu.VMEM((faces, trace, trace), jnp.bfloat16),
                pltpu.VMEM((faces, functionals, trace), jnp.bfloat16),
                pltpu.VMEM((6, 256), jnp.int32),
                pltpu.VMEM((6, 256), jnp.int32),
                pltpu.SMEM((1, devices), jnp.int32),
                pltpu.VMEM((8, 128), jnp.int32),
                pltpu.VMEM((8, 128), jnp.int32),
                pltpu.SMEM((8, 128), jnp.int32),
                pltpu.SMEM((8, 128), jnp.int32),
                pltpu.VMEM((48, 128), jnp.int32),
                pltpu.VMEM((48, 128), jnp.int32),
                pltpu.VMEM((48, 128), jnp.int32),
                pltpu.VMEM((28, 16, 128), jnp.bfloat16),
                pltpu.VMEM((faces, functionals, trace), jnp.float32),
                pltpu.VMEM((LIVE, 16, 768), jnp.bfloat16),
                pltpu.VMEM((REMOTE, 16, 256), jnp.bfloat16),
                pltpu.VMEM((LIVE, 7, 16, 128), jnp.float32),
                pltpu.VMEM((REMOTE + 1, 7, 16, 128), jnp.float32),
                pltpu.VMEM((ZERO_ROW + 1, 16, 128), jnp.bfloat16),
                pltpu.VMEM((20, 16, 128), jnp.bfloat16),
                pltpu.VMEM((20, 16, 128), jnp.bfloat16),
                pltpu.VMEM((20, 16, 128), jnp.bfloat16),
                pltpu.VMEM((20, 16, 128), jnp.bfloat16),
                pltpu.VMEM((8, 16, 128), jnp.bfloat16),
                pltpu.VMEM((8, 16, 128), jnp.bfloat16),
                pltpu.VMEM((8, 16, 128), jnp.bfloat16),
                pltpu.VMEM((13, trace, 256), jnp.bfloat16),
                pltpu.SemaphoreType.DMA((6,)),
                pltpu.SemaphoreType.DMA((4,)),
                pltpu.SemaphoreType.DMA((2, 4)),
                pltpu.SemaphoreType.DMA((2,)),
            ],
            compiler_params=pltpu.CompilerParams(collective_id=0, has_side_effects=True),
        )(elem_mats, face_blocks, rhs, elem_faces.T, orient.T, counts.reshape(1, -1))

    in_specs = (P("elem", None, None), P("elem", None, None), P("elem", None, None), P(), P(), P())
    return jax.shard_map(
        per_device, mesh=mesh, in_specs=in_specs, out_specs=P("elem", None, None), check_vma=False
    )
```

```python
import functools

import jax
import jax.numpy as jnp
from jax import lax
from jax.experimental import pallas as pl
from jax.experimental.pallas import tpu as pltpu
from jax.sharding import PartitionSpec as P

EDGE = 5
TRACE = 125
SLOT = 4
LIVE = 9
ARRIVED = 72
ZERO_ROW = 92
WINDOW = 142
REMOTE = 16
PICK_BACK = 80
PICK_OUT = 84
QUEUE = 88
ROUTES = (0, 1, 3, 4)
SEMS = (0, 1, None, 2, 3)
PLANE = 32
MESH = pl.DeviceIdType.MESH


def lanes_of(values, index):
    return jnp.take_along_axis(values, index, axis=1, mode="promise_in_bounds")


def code_tables():
    shape = (48, 128)
    row = lax.broadcasted_iota(jnp.int32, shape, 0)
    lane = lax.broadcasted_iota(jnp.int32, shape, 1)
    side, code = row >> 3, row & 7

    def split(i):
        comp = (i * 1311) >> 15
        rest = i - comp * 25
        first = (rest * 205) >> 10
        return comp, first, rest - first * 5

    swap, flip_p, flip_q = (code & 4) > 0, (code & 1) > 0, (code & 2) > 0
    low = lane + 3 * side
    high = lane - (128 - 3 * side)
    node = jnp.where(low < TRACE, low, jnp.where(high >= 0, high, 0))
    comp, p, q = split(node)
    p, q = jnp.where(swap, q, p), jnp.where(swap, p, q)
    p = jnp.where(flip_p, EDGE - 1 - p, p)
    q = jnp.where(flip_q, EDGE - 1 - q, q)
    forward = comp * 25 + p * 5 + q
    comp, p, q = split(jnp.minimum(lane, TRACE - 1))
    p = jnp.where(flip_p, EDGE - 1 - p, p)
    q = jnp.where(flip_q, EDGE - 1 - q, q)
    p, q = jnp.where(swap, q, p), jnp.where(swap, p, q)
    backward = (comp * 25 + p * 5 + q + TRACE * side) & 127
    skew = row_skew(side)
    node = jnp.where(lane >= skew, lane - skew, lane + 128 - skew)
    comp, p, q = split(jnp.where(node < TRACE, node, 0))
    p, q = jnp.where(swap, q, p), jnp.where(swap, p, q)
    p = jnp.where(flip_p, EDGE - 1 - p, p)
    q = jnp.where(flip_q, EDGE - 1 - q, q)
    skewed = comp * 25 + p * 5 + q
    return forward, backward, skewed


def row_start(side):
    return jnp.where(side == 5, 608, ((TRACE * side) >> 4) << 4)


def row_skew(side):
    return TRACE * side - row_start(side)


def index_tables(me, devices, right_first, faces, codes, shift, count_of):
    shape = (8, 128)
    row = lax.broadcasted_iota(jnp.int32, shape, 0)
    lane = lax.broadcasted_iota(jnp.int32, shape, 1)
    packed = faces * 8 + codes
    packed = jnp.concatenate([packed, jnp.zeros((2, 256), jnp.int32)], axis=0)
    packed = pltpu.roll(packed, shift, 1)[:, :128]
    take = jnp.minimum(12 * row + (lane >> 3), 127)
    flat = jnp.zeros(shape, jnp.int32)
    for k in range(6):
        source = jnp.broadcast_to(packed[k : k + 1, :], shape)
        flat = jnp.where((lane & 7) == k, lanes_of(source, take), flat)
    face = flat >> 3
    owner = (face * 9710) >> 18
    local = face - owner * 27
    device = row + (me - 2)
    count = jnp.zeros(shape, jnp.int32)
    for r in range(5):
        count = jnp.where(row == r, count_of[r], count)
    live = (
        ((lane >> 3) < count)
        & ((lane & 7) < 6)
        & (row < 5)
        & (device >= 0)
        & (device < devices)
    )
    key = jnp.where(live, owner, -9)
    mine_key = jnp.broadcast_to(key[2:3, :], shape)
    mine_local = jnp.broadcast_to(local[2:3, :], shape)
    mine_code = jnp.broadcast_to(flat[2:3, :] & 7, shape)
    sends = (mine_key == device) & (row < 5)
    takes = (key == me) & (row != 2)
    sent = jnp.where(sends & (row != 2), 1, 0)
    in_first = jnp.where((row > 2) == right_first, sent, 0)
    firsts = jnp.broadcast_to(jnp.sum(in_first, axis=0, keepdims=True), shape)
    remote = jnp.broadcast_to(jnp.sum(sent, axis=0, keepdims=True), shape)
    seconds = remote - firsts
    lists = jnp.where(row == 5, firsts, jnp.where(row == 6, seconds, 0))
    upper = jnp.where(row >= 5, lists, jnp.where(sends, 1, 0))
    both = jnp.concatenate([upper, takes.astype(jnp.int32)], axis=0)
    lane16 = lax.broadcasted_iota(jnp.int32, (16, 128), 1)
    rank = both
    for step in (1, 2, 4, 8, 16, 32, 64):
        rank = rank + jnp.where(lane16 >= step, pltpu.roll(rank, step, 1), 0)
    rank = rank - both
    send_rank, take_rank = rank[:8], rank[8:]
    place = jnp.where(mine_key == me, mine_local, 27)
    side = lane & 7
    code = side * 8 + mine_code
    order = jnp.where(
        firsts > 0,
        jnp.broadcast_to(send_rank[5:6, :], shape),
        REMOTE // 2 + jnp.broadcast_to(send_rank[6:7, :], shape),
    )
    base = jnp.where(row > 2, SLOT * (row - 3), SLOT * row)
    slot = jnp.sum(jnp.where(sent > 0, base + send_rank, 0), axis=0, keepdims=True)
    slot = jnp.broadcast_to(slot, shape)
    inner = lists
    for step in (1, 2, 4):
        inner = inner + jnp.where(side >= step, pltpu.roll(inner, step, 1), 0)
    earlier = jnp.where(
        firsts > 0,
        jnp.broadcast_to(inner[5:6, :], shape),
        jnp.broadcast_to(inner[6:7, :], shape),
    )
    element = lane >> 3
    adds = jnp.where(earlier == 1, 0, 1)
    field = slot | (code << 5) | (element << 11) | ((row_start(side) >> 4) << 15)
    field = field | (row_skew(side) << 21) | (adds << 26)
    queue = jnp.where(remote > 0, order, -1)
    last = jnp.where(row == 6, REMOTE // 2, 0) + send_rank
    last = jnp.where((side == 7) & (inner > 0), last, 0)
    for step in (1, 2, 4):
        last = last + pltpu.roll(last, 128 - step, 1)
    last_one = jnp.broadcast_to(last[5:6, :], shape)
    last_two = jnp.broadcast_to(last[6:7, :], shape)
    packed = code | (element << 8) | (last_one << 16) | (last_two << 24)
    first = jnp.where(row == 0, place, packed)
    values = jnp.concatenate([packed, local], axis=0)
    slot_of = jnp.where(both > 0, rank, -1)
    for s in range(SLOT):
        found = jnp.sum(jnp.where(slot_of == s, values, 0), axis=1, keepdims=True)
        first = jnp.where(lane == PICK_OUT + s, found[:8], first)
        first = jnp.where(lane == PICK_BACK + s, found[8:], first)
    for t in range(2):
        found = jnp.sum(jnp.where(queue == row + 8 * t, field, 0), axis=1, keepdims=True)
        first = jnp.where(lane == QUEUE + t, found, first)

    home = jnp.where(mine_key == me, local, -1)
    match = jnp.where(row == 2, home, jnp.where(takes, local, -1))
    source = jnp.where(row == 2, lane, ARRIVED + SLOT * row + take_rank)
    second = jnp.zeros(shape, jnp.int32)
    for t in range(4):
        own = row + 8 * t
        most = jnp.full(shape, -1, jnp.int32)
        least = jnp.full(shape, 999, jnp.int32)
        for r in range(5):
            same = jnp.broadcast_to(match[r : r + 1, :], shape) == own
            value = jnp.broadcast_to(source[r : r + 1, :], shape)
            most = jnp.maximum(most, jnp.where(same, value, -1))
            least = jnp.minimum(least, jnp.where(same, value, 999))
        most = jnp.max(most, axis=1, keepdims=True)
        least = jnp.min(least, axis=1, keepdims=True)
        one = jnp.where(most < 0, ZERO_ROW, most)
        two = jnp.where(least >= most, ZERO_ROW, least)
        second = jnp.where(lane == 2 * t, one, jnp.where(lane == 2 * t + 1, two, second))
    return first, second


def kernel(
    devices,
    mats_hbm, blocks_hbm, rhs_hbm, faces_hbm, codes_hbm, counts_hbm,
    out_ref,
    mats, blocks, rhs, faces, codes, counts,
    first_v, second_v, first_s, second_s, forward, backward, skewed,
    table, solved, frames, shifted, home, sums, terms, send_one, recv_one, send_two, recv_two,
    relay, held_one, held_two, pairs, load_sem, send_sem, recv_sem, relay_sem,
):
    me = lax.axis_index("elem")
    barrier = pltpu.get_barrier_semaphore()

    def greet(signals):
        for wanted, peer in signals:

            @pl.when(wanted)
            def _(peer=peer):
                pl.semaphore_signal(
                    barrier, inc=1, device_id=(peer,), device_id_type=MESH
                )

    place = lax.rem(me, PLANE)
    late = (place >= PLANE - 2) & (me < devices - PLANE)
    late_one = (place == PLANE - 1) & (me < devices - PLANE)
    early = (place < 2) & (me >= PLANE)
    early_zero = (place == 0) & (me >= PLANE)
    relays = (place >= PLANE - 8) & (place < PLANE - 6) & (me >= PLANE)
    relays_zero = (place == PLANE - 8) & (me >= PLANE)
    greet([(relays, me - 24), (late, me + 26), (late_one, me + 25)])
    start = 12 * me - 24
    base = pl.multiple_of(jnp.clip((start // 128) * 128, 0, faces_hbm.shape[1] - 256), 128)
    shift = (256 - (start - base)) % 256
    window = pl.ds(base, 256)
    loads = [
        pltpu.make_async_copy(faces_hbm.at[:, window], faces, load_sem.at[0]),
        pltpu.make_async_copy(codes_hbm.at[:, window], codes, load_sem.at[1]),
        pltpu.make_async_copy(counts_hbm, counts, load_sem.at[2]),
        pltpu.make_async_copy(rhs_hbm, rhs, load_sem.at[3]),
        pltpu.make_async_copy(blocks_hbm, blocks, load_sem.at[4]),
    ]
    for load in loads:
        load.start()
    peers = [me + (r - 2) for r in range(5)]
    exists = [(me >= 2 - r) if r < 2 else (me < devices + 2 - r) for r in range(5)]
    greets = list(exists)
    greets[3] = exists[3] & jnp.logical_not(late_one)
    greets[4] = exists[4] & jnp.logical_not(late)
    direct = list(exists)
    direct[0] = exists[0] & jnp.logical_not(early)
    direct[1] = exists[1] & jnp.logical_not(early_zero)
    right_first = lax.rem(me // 2, 4) == 0
    greet([(greets[r], peers[r]) for r in ROUTES])
    heard = 4 - jnp.maximum(2 - me, 0) - jnp.maximum(me - (devices - 3), 0)
    heard = heard - early_zero.astype(jnp.int32)
    heard = heard + relays.astype(jnp.int32) + relays_zero.astype(jnp.int32)
    mat_loads = [
        pltpu.make_async_copy(
            mats_hbm.at[pl.ds(3 * c, 3)], mats.at[pl.ds(3 * c, 3)], load_sem.at[c]
        )
        for c in range(3)
    ]

    table[...] = jnp.zeros_like(table)
    terms[...] = jnp.zeros_like(terms)
    pairs[...] = jnp.zeros_like(pairs)
    sums[0] = jnp.zeros_like(sums[0])
    forward[...], backward[...], skewed[...] = code_tables()

    for load in loads[:3]:
        load.wait()
    for load in mat_loads:
        load.start()
    count_of = [counts[0, jnp.clip(me - 2 + r, 0, devices - 1)] for r in range(5)]
    first_v[...], second_v[...] = index_tables(
        me, devices, right_first, faces[...], codes[...], shift, count_of
    )
    tables = [
        pltpu.make_async_copy(first_v, first_s, load_sem.at[5]),
        pltpu.make_async_copy(second_v, second_s, load_sem.at[3]),
    ]
    tables[0].start()

    loads[3].wait()
    tables[1].start()
    loads[4].wait()
    for f in range(27):
        value = jnp.dot(rhs[f], blocks[f], preferred_element_type=jnp.float32)
        solved[f] = value
        table[f, :, :TRACE] = value.astype(jnp.bfloat16)

    tables[0].wait()

    def route(send, recv, leg, r, slot):
        return pltpu.make_async_remote_copy(
            src_ref=send.at[pl.ds(SLOT * r, SLOT)],
            dst_ref=recv.at[pl.ds(SLOT * slot, SLOT)],
            send_sem=send_sem.at[SEMS[r]],
            recv_sem=recv_sem.at[leg, SEMS[slot]],
            device_id=(peers[r],),
            device_id_type=MESH,
        )

    def exchange(send, recv, leg, sends, routes=ROUTES):
        for r in routes:

            @pl.when(sends[r])
            def _(r=r):
                route(send, recv, leg, r, 4 - r).start()

    def to_relay(r):
        return pltpu.make_async_remote_copy(
            src_ref=send_one.at[pl.ds(SLOT * r, SLOT)],
            dst_ref=relay.at[pl.ds(SLOT * r, SLOT)],
            send_sem=send_sem.at[r],
            recv_sem=relay_sem.at[r],
            device_id=(me + 24,),
            device_id_type=MESH,
        )

    def onward(r):
        return pltpu.make_async_remote_copy(
            src_ref=relay.at[pl.ds(SLOT * r, SLOT)],
            dst_ref=recv_one.at[pl.ds(SLOT * (4 - r), SLOT)],
            send_sem=load_sem.at[3 + r],
            recv_sem=recv_sem.at[0, SEMS[4 - r]],
            device_id=(me - 26 + r,),
            device_id_type=MESH,
        )

    def when_each(conditions, act):
        for r, wanted in enumerate(conditions):

            @pl.when(wanted)
            def _(r=r):
                act(r)

    def settle(send, recv, leg, routes, wanted=True):
        for r in routes:

            @pl.when(exists[r] & wanted)
            def _(r=r):
                route(send, recv, leg, r, r).wait_recv()

    for r in ROUTES:
        for s in range(SLOT):
            send_one[SLOT * r + s] = table[first_s[r, PICK_BACK + s]]
    pl.semaphore_wait(barrier, heard)
    when_each((early, early_zero), lambda r: to_relay(r).start())
    exchange(send_one, recv_one, 0, direct)
    tables[1].wait()

    def forward_on(r):
        to_relay(r).wait_recv()
        onward(r).start()

    lane = lax.broadcasted_iota(jnp.int32, (16, 128), 1)

    def turned(value, codes_ref, code):
        index = codes_ref[pl.ds(code, 1), :]
        return lanes_of(value, jnp.broadcast_to(index, (16, 128)))

    for e in range(LIVE):
        pieces = []
        for k in range(6):
            value = table[first_s[0, 8 * e + k]].astype(jnp.float32)
            pieces.append(turned(value, forward, first_s[1, 8 * e + k] & 255))
        pieces.append(jnp.zeros((16, 128), jnp.float32))
        for c in range(6):
            column = jnp.where(lane < TRACE - 3 * c, pieces[c], pieces[c + 1])
            frames[e, :, 128 * c : 128 * (c + 1)] = column.astype(jnp.bfloat16)

    def columns(ref, at, value):
        for c in range(5):
            ref[at, c + 1] = value[:, 128 * c : 128 * (c + 1)]
        ref[at, 6, :, :110] = value[:, 640:750]

    def apply(e, carry):
        value = jnp.dot(frames[e, :, :750], mats[e], preferred_element_type=jnp.float32)
        columns(home, e, value)
        return carry

    when_each((relays, relays_zero), forward_on)
    mat_loads[0].wait()
    lax.fori_loop(0, 3, apply, 0)
    mat_loads[1].wait()
    lax.fori_loop(3, 4, apply, 0)
    lax.fori_loop(4, 6, apply, 0)
    mat_loads[2].wait()
    lax.fori_loop(6, LIVE, apply, 0)

    when_each((early, early_zero), lambda r: to_relay(r).wait_send())
    for r in ROUTES:

        @pl.when(direct[r])
        def _(r=r):
            route(send_one, recv_one, 0, r, 4 - r).wait_send()

    total = None
    for q in range(REMOTE):
        if q == 0:
            settle(send_one, recv_one, 0, (3, 4), right_first)
            settle(send_one, recv_one, 0, (0, 1), jnp.logical_not(right_first))
            held_one[...] = recv_one[pl.ds(jnp.where(right_first, 12, 0), 8)]
        if q == REMOTE // 2:
            settle(send_one, recv_one, 0, (0, 1), right_first)
            settle(send_one, recv_one, 0, (3, 4), jnp.logical_not(right_first))
            held_two[...] = recv_one[pl.ds(jnp.where(right_first, 0, 12), 8)]
            total = None
        word = first_s[q % 8, QUEUE + q // 8]
        held = held_one if q < REMOTE // 2 else held_two
        skew = (word >> 21) & 31
        value = held[word & 31].astype(jnp.float32)
        value = turned(value, skewed, (word >> 5) & 63)
        node = lane - skew
        main = jnp.where((node >= 0) & (node < TRACE), value, 0.0)
        rest = jnp.where(lane <= skew - 4, value, 0.0)
        shifted[q, :, :128] = main.astype(jnp.bfloat16)
        shifted[q, :, 128:] = rest.astype(jnp.bfloat16)
        rows = pl.ds(((word >> 15) & 63) * 16, WINDOW)
        part = jnp.dot(
            shifted[q, :, :WINDOW],
            mats[(word >> 11) & 15, rows, :],
            preferred_element_type=jnp.float32,
        )
        adds = (word >> 26).astype(jnp.float32)
        total = part if total is None else part + total * adds
        columns(sums, q + 1, total)

    def term(word):
        code, e = word & 255, (word >> 8) & 255
        one, two = (word >> 16) & 255, word >> 24
        k = code >> 3
        value = jnp.where(
            lane < TRACE - 3 * k,
            home[e, k + 1] + (sums[one, k + 1] + sums[two, k + 1]),
            home[e, k] + (sums[one, k] + sums[two, k]),
        )
        value = value.astype(jnp.bfloat16).astype(jnp.float32)
        return turned(value, backward, code).astype(jnp.bfloat16)

    def partials(r):
        for s in range(SLOT):
            send_two[SLOT * r + s] = term(first_s[r, PICK_OUT + s])

    for r in (4, 3):
        partials(r)
    exchange(send_two, recv_two, 1, exists, (4, 3))
    for r in (1, 0):
        partials(r)
    exchange(send_two, recv_two, 1, exists, (1, 0))

    for e in range(LIVE):
        for k in range(6):
            terms[8 * e + k] = term(first_s[1, 8 * e + k])

    for f in range(26):
        column = 128 * (f % 2)
        pairs[f // 2, :, column : column + TRACE] = blocks[f]

    when_each((relays, relays_zero), lambda r: onward(r).wait_send())
    for side in ((4, 3), (1, 0)):
        settle(send_two, recv_two, 1, side)
        for r in side:
            terms[ARRIVED + SLOT * r : ARRIVED + SLOT * (r + 1)] = recv_two[
                SLOT * r : SLOT * (r + 1)
            ]

    def residual(f):
        one, two = second_s[f % 8, 2 * (f // 8)], second_s[f % 8, 2 * (f // 8) + 1]
        summed = terms[one].astype(jnp.float32) + terms[two].astype(jnp.float32)
        return (rhs[f].astype(jnp.float32) - summed[:, :TRACE]).astype(jnp.bfloat16)

    for f in range(0, 26, 2):
        both = jnp.concatenate([residual(f), residual(f + 1)], axis=0)
        step = jnp.dot(both, pairs[f // 2], preferred_element_type=jnp.float32)
        out_ref[f] = solved[f] + step[:16, :TRACE]
        out_ref[f + 1] = solved[f + 1] + step[16:, 128 : 128 + TRACE]
    out_ref[26] = solved[26] + jnp.dot(
        residual(26), blocks[26], preferred_element_type=jnp.float32
    )
    for r in ROUTES:

        @pl.when(exists[r])
        def _(r=r):
            route(send_two, recv_two, 1, r, 4 - r).wait_send()


def solution(mesh):
    devices = mesh.shape["elem"]

    def per_device(elem_mats, face_blocks, rhs, elem_faces, orient, counts):
        faces, functionals, trace = rhs.shape
        return pl.pallas_call(
            functools.partial(kernel, devices),
            name="sweeps",
            out_shape=pltpu.VMEM(rhs.shape, jnp.float32),
            in_specs=[pl.BlockSpec(memory_space=pl.ANY)] * 6,
            out_specs=pl.BlockSpec(memory_space=pltpu.VMEM),
            scratch_shapes=[
                pltpu.VMEM((LIVE, 750, 750), jnp.bfloat16),
                pltpu.VMEM((faces, trace, trace), jnp.bfloat16),
                pltpu.VMEM((faces, functionals, trace), jnp.bfloat16),
                pltpu.VMEM((6, 256), jnp.int32),
                pltpu.VMEM((6, 256), jnp.int32),
                pltpu.SMEM((1, devices), jnp.int32),
                pltpu.VMEM((8, 128), jnp.int32),
                pltpu.VMEM((8, 128), jnp.int32),
                pltpu.SMEM((8, 128), jnp.int32),
                pltpu.SMEM((8, 128), jnp.int32),
                pltpu.VMEM((48, 128), jnp.int32),
                pltpu.VMEM((48, 128), jnp.int32),
                pltpu.VMEM((48, 128), jnp.int32),
                pltpu.VMEM((28, 16, 128), jnp.bfloat16),
                pltpu.VMEM((faces, functionals, trace), jnp.float32),
                pltpu.VMEM((LIVE, 16, 768), jnp.bfloat16),
                pltpu.VMEM((REMOTE, 16, 256), jnp.bfloat16),
                pltpu.VMEM((LIVE, 7, 16, 128), jnp.float32),
                pltpu.VMEM((REMOTE + 1, 7, 16, 128), jnp.float32),
                pltpu.VMEM((ZERO_ROW + 1, 16, 128), jnp.bfloat16),
                pltpu.VMEM((20, 16, 128), jnp.bfloat16),
                pltpu.VMEM((20, 16, 128), jnp.bfloat16),
                pltpu.VMEM((20, 16, 128), jnp.bfloat16),
                pltpu.VMEM((20, 16, 128), jnp.bfloat16),
                pltpu.VMEM((8, 16, 128), jnp.bfloat16),
                pltpu.VMEM((8, 16, 128), jnp.bfloat16),
                pltpu.VMEM((8, 16, 128), jnp.bfloat16),
                pltpu.VMEM((13, trace, 256), jnp.bfloat16),
                pltpu.SemaphoreType.DMA((6,)),
                pltpu.SemaphoreType.DMA((4,)),
                pltpu.SemaphoreType.DMA((2, 4)),
                pltpu.SemaphoreType.DMA((2,)),
            ],
            compiler_params=pltpu.CompilerParams(collective_id=0, has_side_effects=True),
        )(elem_mats, face_blocks, rhs, elem_faces.T, orient.T, counts.reshape(1, -1))

    in_specs = (P("elem", None, None), P("elem", None, None), P("elem", None, None), P(), P(), P())
    return jax.shard_map(
        per_device, mesh=mesh, in_specs=in_specs, out_specs=P("elem", None, None), check_vma=False
    )
```

```python
import functools

import jax
import jax.numpy as jnp
from jax import lax
from jax.experimental import pallas as pl
from jax.experimental.pallas import tpu as pltpu
from jax.sharding import PartitionSpec as P

EDGE = 5
TRACE = 125
SLOT = 4
LIVE = 9
ARRIVED = 72
ZERO_ROW = 92
WINDOW = 142
REMOTE = 16
PICK_BACK = 80
PICK_OUT = 84
QUEUE = 88
ROUTES = (0, 1, 3, 4)
SEMS = (0, 1, None, 2, 3)
PLANE = 32
MESH = pl.DeviceIdType.MESH


def lanes_of(values, index):
    return jnp.take_along_axis(values, index, axis=1, mode="promise_in_bounds")


def code_tables():
    shape = (48, 128)
    row = lax.broadcasted_iota(jnp.int32, shape, 0)
    lane = lax.broadcasted_iota(jnp.int32, shape, 1)
    side, code = row >> 3, row & 7

    def split(i):
        comp = (i * 1311) >> 15
        rest = i - comp * 25
        first = (rest * 205) >> 10
        return comp, first, rest - first * 5

    swap, flip_p, flip_q = (code & 4) > 0, (code & 1) > 0, (code & 2) > 0
    low = lane + 3 * side
    high = lane - (128 - 3 * side)
    node = jnp.where(low < TRACE, low, jnp.where(high >= 0, high, 0))
    comp, p, q = split(node)
    p, q = jnp.where(swap, q, p), jnp.where(swap, p, q)
    p = jnp.where(flip_p, EDGE - 1 - p, p)
    q = jnp.where(flip_q, EDGE - 1 - q, q)
    forward = comp * 25 + p * 5 + q
    comp, p, q = split(jnp.minimum(lane, TRACE - 1))
    p = jnp.where(flip_p, EDGE - 1 - p, p)
    q = jnp.where(flip_q, EDGE - 1 - q, q)
    p, q = jnp.where(swap, q, p), jnp.where(swap, p, q)
    backward = (comp * 25 + p * 5 + q + TRACE * side) & 127
    skew = row_skew(side)
    node = jnp.where(lane >= skew, lane - skew, lane + 128 - skew)
    comp, p, q = split(jnp.where(node < TRACE, node, 0))
    p, q = jnp.where(swap, q, p), jnp.where(swap, p, q)
    p = jnp.where(flip_p, EDGE - 1 - p, p)
    q = jnp.where(flip_q, EDGE - 1 - q, q)
    skewed = comp * 25 + p * 5 + q
    return forward, backward, skewed


def row_start(side):
    return jnp.where(side == 5, 608, ((TRACE * side) >> 4) << 4)


def row_skew(side):
    return TRACE * side - row_start(side)


def index_tables(me, devices, right_first, faces, codes, shift, count_of):
    shape = (8, 128)
    row = lax.broadcasted_iota(jnp.int32, shape, 0)
    lane = lax.broadcasted_iota(jnp.int32, shape, 1)
    packed = faces * 8 + codes
    packed = jnp.concatenate([packed, jnp.zeros((2, 256), jnp.int32)], axis=0)
    packed = pltpu.roll(packed, shift, 1)[:, :128]
    take = jnp.minimum(12 * row + (lane >> 3), 127)
    flat = jnp.zeros(shape, jnp.int32)
    for k in range(6):
        source = jnp.broadcast_to(packed[k : k + 1, :], shape)
        flat = jnp.where((lane & 7) == k, lanes_of(source, take), flat)
    face = flat >> 3
    owner = (face * 9710) >> 18
    local = face - owner * 27
    device = row + (me - 2)
    count = jnp.zeros(shape, jnp.int32)
    for r in range(5):
        count = jnp.where(row == r, count_of[r], count)
    live = (
        ((lane >> 3) < count)
        & ((lane & 7) < 6)
        & (row < 5)
        & (device >= 0)
        & (device < devices)
    )
    key = jnp.where(live, owner, -9)
    mine_key = jnp.broadcast_to(key[2:3, :], shape)
    mine_local = jnp.broadcast_to(local[2:3, :], shape)
    mine_code = jnp.broadcast_to(flat[2:3, :] & 7, shape)
    sends = (mine_key == device) & (row < 5)
    takes = (key == me) & (row != 2)
    sent = jnp.where(sends & (row != 2), 1, 0)
    in_first = jnp.where((row > 2) == right_first, sent, 0)
    firsts = jnp.broadcast_to(jnp.sum(in_first, axis=0, keepdims=True), shape)
    remote = jnp.broadcast_to(jnp.sum(sent, axis=0, keepdims=True), shape)
    seconds = remote - firsts
    lists = jnp.where(row == 5, firsts, jnp.where(row == 6, seconds, 0))
    upper = jnp.where(row >= 5, lists, jnp.where(sends, 1, 0))
    both = jnp.concatenate([upper, takes.astype(jnp.int32)], axis=0)
    lane16 = lax.broadcasted_iota(jnp.int32, (16, 128), 1)
    rank = both
    for step in (1, 2, 4, 8, 16, 32, 64):
        rank = rank + jnp.where(lane16 >= step, pltpu.roll(rank, step, 1), 0)
    rank = rank - both
    send_rank, take_rank = rank[:8], rank[8:]
    place = jnp.where(mine_key == me, mine_local, 27)
    side = lane & 7
    code = side * 8 + mine_code
    order = jnp.where(
        firsts > 0,
        jnp.broadcast_to(send_rank[5:6, :], shape),
        REMOTE // 2 + jnp.broadcast_to(send_rank[6:7, :], shape),
    )
    base = jnp.where(row > 2, SLOT * (row - 3), SLOT * row)
    slot = jnp.sum(jnp.where(sent > 0, base + send_rank, 0), axis=0, keepdims=True)
    slot = jnp.broadcast_to(slot, shape)
    inner = lists
    for step in (1, 2, 4):
        inner = inner + jnp.where(side >= step, pltpu.roll(inner, step, 1), 0)
    earlier = jnp.where(
        firsts > 0,
        jnp.broadcast_to(inner[5:6, :], shape),
        jnp.broadcast_to(inner[6:7, :], shape),
    )
    element = lane >> 3
    adds = jnp.where(earlier == 1, 0, 1)
    field = slot | (code << 5) | (element << 11) | ((row_start(side) >> 4) << 15)
    field = field | (row_skew(side) << 21) | (adds << 26)
    queue = jnp.where(remote > 0, order, -1)
    last = jnp.where(row == 6, REMOTE // 2, 0) + send_rank
    last = jnp.where((side == 7) & (inner > 0), last, 0)
    for step in (1, 2, 4):
        last = last + pltpu.roll(last, 128 - step, 1)
    last_one = jnp.broadcast_to(last[5:6, :], shape)
    last_two = jnp.broadcast_to(last[6:7, :], shape)
    packed = code | (element << 8) | (last_one << 16) | (last_two << 24)
    first = jnp.where(row == 0, place, packed)
    values = jnp.concatenate([packed, local], axis=0)
    slot_of = jnp.where(both > 0, rank, -1)
    for s in range(SLOT):
        found = jnp.sum(jnp.where(slot_of == s, values, 0), axis=1, keepdims=True)
        first = jnp.where(lane == PICK_OUT + s, found[:8], first)
        first = jnp.where(lane == PICK_BACK + s, found[8:], first)
    for t in range(2):
        found = jnp.sum(jnp.where(queue == row + 8 * t, field, 0), axis=1, keepdims=True)
        first = jnp.where(lane == QUEUE + t, found, first)

    home = jnp.where(mine_key == me, local, -1)
    match = jnp.where(row == 2, home, jnp.where(takes, local, -1))
    source = jnp.where(row == 2, lane, ARRIVED + SLOT * row + take_rank)
    second = jnp.zeros(shape, jnp.int32)
    for t in range(4):
        own = row + 8 * t
        most = jnp.full(shape, -1, jnp.int32)
        least = jnp.full(shape, 999, jnp.int32)
        for r in range(5):
            same = jnp.broadcast_to(match[r : r + 1, :], shape) == own
            value = jnp.broadcast_to(source[r : r + 1, :], shape)
            most = jnp.maximum(most, jnp.where(same, value, -1))
            least = jnp.minimum(least, jnp.where(same, value, 999))
        most = jnp.max(most, axis=1, keepdims=True)
        least = jnp.min(least, axis=1, keepdims=True)
        one = jnp.where(most < 0, ZERO_ROW, most)
        two = jnp.where(least >= most, ZERO_ROW, least)
        second = jnp.where(lane == 2 * t, one, jnp.where(lane == 2 * t + 1, two, second))
    return first, second


def kernel(
    devices,
    mats_hbm, blocks_hbm, rhs_hbm, faces_hbm, codes_hbm, counts_hbm,
    out_ref,
    mats, blocks, rhs, faces, codes, counts,
    first_v, second_v, first_s, second_s, forward, backward, skewed,
    table, solved, frames, shifted, home, sums, terms, send_one, recv_one, send_two, recv_two,
    relay, held_one, held_two, pairs, load_sem, send_sem, recv_sem, relay_sem,
):
    me = lax.axis_index("elem")
    barrier = pltpu.get_barrier_semaphore()

    def greet(signals):
        for wanted, peer in signals:

            @pl.when(wanted)
            def _(peer=peer):
                pl.semaphore_signal(
                    barrier, inc=1, device_id=(peer,), device_id_type=MESH
                )

    place = lax.rem(me, PLANE)
    late = (place >= PLANE - 2) & (me < devices - PLANE)
    late_one = (place == PLANE - 1) & (me < devices - PLANE)
    early = (place < 2) & (me >= PLANE)
    early_zero = (place == 0) & (me >= PLANE)
    relays = (place >= PLANE - 8) & (place < PLANE - 6) & (me >= PLANE)
    relays_zero = (place == PLANE - 8) & (me >= PLANE)
    greet([(relays, me - 24), (late, me + 26), (late_one, me + 25)])
    start = 12 * me - 24
    base = pl.multiple_of(jnp.clip((start // 128) * 128, 0, faces_hbm.shape[1] - 256), 128)
    shift = (256 - (start - base)) % 256
    window = pl.ds(base, 256)
    loads = [
        pltpu.make_async_copy(faces_hbm.at[:, window], faces, load_sem.at[0]),
        pltpu.make_async_copy(codes_hbm.at[:, window], codes, load_sem.at[1]),
        pltpu.make_async_copy(counts_hbm, counts, load_sem.at[2]),
        pltpu.make_async_copy(rhs_hbm, rhs, load_sem.at[3]),
        pltpu.make_async_copy(blocks_hbm, blocks, load_sem.at[4]),
    ]
    for load in loads:
        load.start()
    peers = [me + (r - 2) for r in range(5)]
    exists = [(me >= 2 - r) if r < 2 else (me < devices + 2 - r) for r in range(5)]
    greets = list(exists)
    greets[3] = exists[3] & jnp.logical_not(late_one)
    greets[4] = exists[4] & jnp.logical_not(late)
    direct = list(exists)
    direct[0] = exists[0] & jnp.logical_not(early)
    direct[1] = exists[1] & jnp.logical_not(early_zero)
    right_first = lax.rem(me // 2, 4) == 0
    greet([(greets[r], peers[r]) for r in ROUTES])
    heard = 4 - jnp.maximum(2 - me, 0) - jnp.maximum(me - (devices - 3), 0)
    heard = heard - early_zero.astype(jnp.int32)
    heard = heard + relays.astype(jnp.int32) + relays_zero.astype(jnp.int32)
    mat_loads = [
        pltpu.make_async_copy(
            mats_hbm.at[pl.ds(3 * c, 3)], mats.at[pl.ds(3 * c, 3)], load_sem.at[c]
        )
        for c in range(3)
    ]

    table[...] = jnp.zeros_like(table)
    terms[...] = jnp.zeros_like(terms)
    pairs[...] = jnp.zeros_like(pairs)
    sums[0] = jnp.zeros_like(sums[0])
    forward[...], backward[...], skewed[...] = code_tables()

    for load in loads[:3]:
        load.wait()
    count_of = [counts[0, jnp.clip(me - 2 + r, 0, devices - 1)] for r in range(5)]
    first_v[...], second_v[...] = index_tables(
        me, devices, right_first, faces[...], codes[...], shift, count_of
    )
    tables = [
        pltpu.make_async_copy(first_v, first_s, load_sem.at[5]),
        pltpu.make_async_copy(second_v, second_s, load_sem.at[3]),
    ]
    tables[0].start()
    for load in mat_loads:
        load.start()

    loads[3].wait()
    tables[1].start()
    loads[4].wait()
    for f in range(27):
        value = jnp.dot(rhs[f], blocks[f], preferred_element_type=jnp.float32)
        solved[f] = value
        table[f, :, :TRACE] = value.astype(jnp.bfloat16)

    tables[0].wait()

    def route(send, recv, leg, r, slot):
        return pltpu.make_async_remote_copy(
            src_ref=send.at[pl.ds(SLOT * r, SLOT)],
            dst_ref=recv.at[pl.ds(SLOT * slot, SLOT)],
            send_sem=send_sem.at[SEMS[r]],
            recv_sem=recv_sem.at[leg, SEMS[slot]],
            device_id=(peers[r],),
            device_id_type=MESH,
        )

    def exchange(send, recv, leg, sends, routes=ROUTES):
        for r in routes:

            @pl.when(sends[r])
            def _(r=r):
                route(send, recv, leg, r, 4 - r).start()

    def to_relay(r):
        return pltpu.make_async_remote_copy(
            src_ref=send_one.at[pl.ds(SLOT * r, SLOT)],
            dst_ref=relay.at[pl.ds(SLOT * r, SLOT)],
            send_sem=send_sem.at[r],
            recv_sem=relay_sem.at[r],
            device_id=(me + 24,),
            device_id_type=MESH,
        )

    def onward(r):
        return pltpu.make_async_remote_copy(
            src_ref=relay.at[pl.ds(SLOT * r, SLOT)],
            dst_ref=recv_one.at[pl.ds(SLOT * (4 - r), SLOT)],
            send_sem=load_sem.at[3 + r],
            recv_sem=recv_sem.at[0, SEMS[4 - r]],
            device_id=(me - 26 + r,),
            device_id_type=MESH,
        )

    def when_each(conditions, act):
        for r, wanted in enumerate(conditions):

            @pl.when(wanted)
            def _(r=r):
                act(r)

    def settle(send, recv, leg, routes, wanted=True):
        for r in routes:

            @pl.when(exists[r] & wanted)
            def _(r=r):
                route(send, recv, leg, r, r).wait_recv()

    for r in ROUTES:
        for s in range(SLOT):
            send_one[SLOT * r + s] = table[first_s[r, PICK_BACK + s]]
    pl.semaphore_wait(barrier, heard)
    when_each((early, early_zero), lambda r: to_relay(r).start())
    exchange(send_one, recv_one, 0, direct)
    tables[1].wait()

    def forward_on(r):
        to_relay(r).wait_recv()
        onward(r).start()

    lane = lax.broadcasted_iota(jnp.int32, (16, 128), 1)

    def turned(value, codes_ref, code):
        index = codes_ref[pl.ds(code, 1), :]
        return lanes_of(value, jnp.broadcast_to(index, (16, 128)))

    for e in range(LIVE):
        pieces = []
        for k in range(6):
            value = table[first_s[0, 8 * e + k]].astype(jnp.float32)
            pieces.append(turned(value, forward, first_s[1, 8 * e + k] & 255))
        pieces.append(jnp.zeros((16, 128), jnp.float32))
        for c in range(6):
            column = jnp.where(lane < TRACE - 3 * c, pieces[c], pieces[c + 1])
            frames[e, :, 128 * c : 128 * (c + 1)] = column.astype(jnp.bfloat16)

    def columns(ref, at, value):
        for c in range(5):
            ref[at, c + 1] = value[:, 128 * c : 128 * (c + 1)]
        ref[at, 6, :, :110] = value[:, 640:750]

    def apply(e, carry):
        value = jnp.dot(frames[e, :, :750], mats[e], preferred_element_type=jnp.float32)
        columns(home, e, value)
        return carry

    when_each((relays, relays_zero), forward_on)
    mat_loads[0].wait()
    lax.fori_loop(0, 3, apply, 0)
    mat_loads[1].wait()
    lax.fori_loop(3, 4, apply, 0)
    lax.fori_loop(4, 6, apply, 0)
    mat_loads[2].wait()
    lax.fori_loop(6, LIVE, apply, 0)

    when_each((early, early_zero), lambda r: to_relay(r).wait_send())
    for r in ROUTES:

        @pl.when(direct[r])
        def _(r=r):
            route(send_one, recv_one, 0, r, 4 - r).wait_send()

    total = None
    for q in range(REMOTE):
        if q == 0:
            settle(send_one, recv_one, 0, (3, 4), right_first)
            settle(send_one, recv_one, 0, (0, 1), jnp.logical_not(right_first))
            held_one[...] = recv_one[pl.ds(jnp.where(right_first, 12, 0), 8)]
        if q == REMOTE // 2:
            settle(send_one, recv_one, 0, (0, 1), right_first)
            settle(send_one, recv_one, 0, (3, 4), jnp.logical_not(right_first))
            held_two[...] = recv_one[pl.ds(jnp.where(right_first, 0, 12), 8)]
            total = None
        word = first_s[q % 8, QUEUE + q // 8]
        held = held_one if q < REMOTE // 2 else held_two
        skew = (word >> 21) & 31
        value = held[word & 31].astype(jnp.float32)
        value = turned(value, skewed, (word >> 5) & 63)
        node = lane - skew
        main = jnp.where((node >= 0) & (node < TRACE), value, 0.0)
        rest = jnp.where(lane <= skew - 4, value, 0.0)
        shifted[q, :, :128] = main.astype(jnp.bfloat16)
        shifted[q, :, 128:] = rest.astype(jnp.bfloat16)
        rows = pl.ds(((word >> 15) & 63) * 16, WINDOW)
        part = jnp.dot(
            shifted[q, :, :WINDOW],
            mats[(word >> 11) & 15, rows, :],
            preferred_element_type=jnp.float32,
        )
        adds = (word >> 26).astype(jnp.float32)
        total = part if total is None else part + total * adds
        columns(sums, q + 1, total)

    def term(word):
        code, e = word & 255, (word >> 8) & 255
        one, two = (word >> 16) & 255, word >> 24
        k = code >> 3
        value = jnp.where(
            lane < TRACE - 3 * k,
            home[e, k + 1] + (sums[one, k + 1] + sums[two, k + 1]),
            home[e, k] + (sums[one, k] + sums[two, k]),
        )
        value = value.astype(jnp.bfloat16).astype(jnp.float32)
        return turned(value, backward, code).astype(jnp.bfloat16)

    def partials(r):
        for s in range(SLOT):
            send_two[SLOT * r + s] = term(first_s[r, PICK_OUT + s])

    for r in (4, 3, 1):
        partials(r)
    exchange(send_two, recv_two, 1, exists, (4, 3))
    partials(0)
    exchange(send_two, recv_two, 1, exists, (1, 0))

    for e in range(LIVE):
        for k in range(6):
            terms[8 * e + k] = term(first_s[1, 8 * e + k])

    for f in range(26):
        column = 128 * (f % 2)
        pairs[f // 2, :, column : column + TRACE] = blocks[f]

    settle(send_two, recv_two, 1, ROUTES)
    for r in ROUTES:
        terms[ARRIVED + SLOT * r : ARRIVED + SLOT * (r + 1)] = recv_two[SLOT * r : SLOT * (r + 1)]

    def residual(f):
        one, two = second_s[f % 8, 2 * (f // 8)], second_s[f % 8, 2 * (f // 8) + 1]
        summed = terms[one].astype(jnp.float32) + terms[two].astype(jnp.float32)
        return (rhs[f].astype(jnp.float32) - summed[:, :TRACE]).astype(jnp.bfloat16)

    for f in range(0, 26, 2):
        both = jnp.concatenate([residual(f), residual(f + 1)], axis=0)
        step = jnp.dot(both, pairs[f // 2], preferred_element_type=jnp.float32)
        out_ref[f] = solved[f] + step[:16, :TRACE]
        out_ref[f + 1] = solved[f + 1] + step[16:, 128 : 128 + TRACE]
    out_ref[26] = solved[26] + jnp.dot(
        residual(26), blocks[26], preferred_element_type=jnp.float32
    )
    when_each((relays, relays_zero), lambda r: onward(r).wait_send())
    for r in ROUTES:

        @pl.when(exists[r])
        def _(r=r):
            route(send_two, recv_two, 1, r, 4 - r).wait_send()


def solution(mesh):
    devices = mesh.shape["elem"]

    def per_device(elem_mats, face_blocks, rhs, elem_faces, orient, counts):
        faces, functionals, trace = rhs.shape
        return pl.pallas_call(
            functools.partial(kernel, devices),
            name="sweeps",
            out_shape=pltpu.VMEM(rhs.shape, jnp.float32),
            in_specs=[pl.BlockSpec(memory_space=pl.ANY)] * 6,
            out_specs=pl.BlockSpec(memory_space=pltpu.VMEM),
            scratch_shapes=[
                pltpu.VMEM((LIVE, 750, 750), jnp.bfloat16),
                pltpu.VMEM((faces, trace, trace), jnp.bfloat16),
                pltpu.VMEM((faces, functionals, trace), jnp.bfloat16),
                pltpu.VMEM((6, 256), jnp.int32),
                pltpu.VMEM((6, 256), jnp.int32),
                pltpu.SMEM((1, devices), jnp.int32),
                pltpu.VMEM((8, 128), jnp.int32),
                pltpu.VMEM((8, 128), jnp.int32),
                pltpu.SMEM((8, 128), jnp.int32),
                pltpu.SMEM((8, 128), jnp.int32),
                pltpu.VMEM((48, 128), jnp.int32),
                pltpu.VMEM((48, 128), jnp.int32),
                pltpu.VMEM((48, 128), jnp.int32),
                pltpu.VMEM((28, 16, 128), jnp.bfloat16),
                pltpu.VMEM((faces, functionals, trace), jnp.float32),
                pltpu.VMEM((LIVE, 16, 768), jnp.bfloat16),
                pltpu.VMEM((REMOTE, 16, 256), jnp.bfloat16),
                pltpu.VMEM((LIVE, 7, 16, 128), jnp.float32),
                pltpu.VMEM((REMOTE + 1, 7, 16, 128), jnp.float32),
                pltpu.VMEM((ZERO_ROW + 1, 16, 128), jnp.bfloat16),
                pltpu.VMEM((20, 16, 128), jnp.bfloat16),
                pltpu.VMEM((20, 16, 128), jnp.bfloat16),
                pltpu.VMEM((20, 16, 128), jnp.bfloat16),
                pltpu.VMEM((20, 16, 128), jnp.bfloat16),
                pltpu.VMEM((8, 16, 128), jnp.bfloat16),
                pltpu.VMEM((8, 16, 128), jnp.bfloat16),
                pltpu.VMEM((8, 16, 128), jnp.bfloat16),
                pltpu.VMEM((13, trace, 256), jnp.bfloat16),
                pltpu.SemaphoreType.DMA((6,)),
                pltpu.SemaphoreType.DMA((4,)),
                pltpu.SemaphoreType.DMA((2, 4)),
                pltpu.SemaphoreType.DMA((2,)),
            ],
            compiler_params=pltpu.CompilerParams(collective_id=0, has_side_effects=True),
        )(elem_mats, face_blocks, rhs, elem_faces.T, orient.T, counts.reshape(1, -1))

    in_specs = (P("elem", None, None), P("elem", None, None), P("elem", None, None), P(), P(), P())
    return jax.shard_map(
        per_device, mesh=mesh, in_specs=in_specs, out_specs=P("elem", None, None), check_vma=False
    )
```
